32 devices in a mesh: prow: 8 (over z, x), pcol: 4 (over y, core).
Axes of the slice: x: 2, y: 2, z: 4, core: 2. Of those that a mesh axis runs over, the one named last changes fastest.
Arguments:
- matrix: float32 [24, 512, 6, 2048], P(None, 'prow', None, 'pcol'), may hold values from -6 to 6
- pivots: int32 [2, 512], replicated, may hold values from 0 to 12287, as said below
- lower_inv: float32 [2, 512, 512], replicated
- upper_inv: float32 [2, 512, 512], replicated
Outputs:
- factored: float32 [24, 512, 6, 2048], P(None, 'prow', None, 'pcol')
The draws below stay inside these ranges and needn't reach their ends.
Inputs may be any that keep to these rules, and one draw needn't show every extreme that they name: pivots[k, i] is at least k * 512 + i; every panel has one entry equal to 12287, and the first panel's first row keeps its place.
All inputs are finite; a program needn't handle non-finite values.
Results may differ from the reference program's by a relative error of at most 0.00011.
Values sent between devices are 32-bit elements; how exact they have to be, the bound alone decides.
No kernel may reach another device: no remote copies, remote signals or barrier semaphores. Data moves between devices by JAX's collectives and lax.ppermute only.
A program may use at most 128 MiB of HBM per device.

```python
import math
import jax
import jax.numpy as jnp
from jax import lax

M = 12288
NB = 512
PANELS = 2
ROWBLK = 24
COLSPAN = 2048
COLBLK = 6


def draw_pivots(key, part):
    bits_key = jax.random.fold_in(key, 21)
    pick_key = jax.random.fold_in(key, 22)
    starts = jnp.arange(PANELS, dtype=jnp.int32)[:, None] * NB + jnp.arange(NB, dtype=jnp.int32)[None, :]
    random_bits = jax.random.randint(bits_key, (PANELS, NB), 0, 2 ** 30, dtype=jnp.int32)
    chosen = starts + random_bits % (M - starts)
    picked = jax.random.randint(pick_key, (PANELS, 1), 1, NB, dtype=jnp.int32)
    positions = jnp.arange(NB, dtype=jnp.int32)[None, :]
    chosen = jnp.where(positions == picked, M - 1, chosen)
    first_spot = (jnp.arange(PANELS, dtype=jnp.int32)[:, None] == 0) & (positions == 0)
    chosen = jnp.where(first_spot, 0, chosen)
    return chosen.astype(jnp.int32)


def draw_lower_inv(key, part):
    entry_key = jax.random.fold_in(key, 31)
    entries = jax.random.normal(entry_key, (PANELS, NB, NB), jnp.float32)
    row_ids = jnp.arange(NB)[:, None]
    col_ids = jnp.arange(NB)[None, :]
    below = jnp.where(row_ids > col_ids, entries * (0.7 / math.sqrt(NB)), 0.0)
    return (below + jnp.where(row_ids == col_ids, 1.0, 0.0)).astype(jnp.float32)


def draw_upper_inv(key, part):
    entry_key = jax.random.fold_in(key, 41)
    diag_key = jax.random.fold_in(key, 42)
    entries = jax.random.normal(entry_key, (PANELS, NB, NB), jnp.float32)
    diag_vals = jnp.exp(jax.random.uniform(diag_key, (PANELS, NB, NB), jnp.float32, math.log(0.5), math.log(2.0)))
    row_ids = jnp.arange(NB)[:, None]
    col_ids = jnp.arange(NB)[None, :]
    above = jnp.where(row_ids < col_ids, entries * (0.7 / math.sqrt(NB)), 0.0)
    diagonal_part = jnp.where(row_ids == col_ids, diag_vals, 0.0)
    return ((above + diagonal_part) / math.sqrt(NB)).astype(jnp.float32)


def level_of(key, extent, split, least, largest):
    factor_of = 1.0
    for dim, blocks in split:
        draws = jax.random.uniform(jax.random.fold_in(jax.random.fold_in(key, 6), dim), (blocks,), jnp.float32, least / len(split), largest / len(split))
        factor_of = factor_of * jnp.repeat(jnp.exp(draws), extent[dim] // blocks).reshape((-1,) + (1,) * (len(extent) - 1 - dim))
    return factor_of


def bell_draw(rng, dims, width, reach, split=(), held_as=jnp.bfloat16):
    level = level_of(rng, dims, split, -0.22, 0.18) if split else 1.0
    array = jax.random.normal(rng, dims, jnp.float32) * width * level
    return jnp.minimum(jnp.maximum(array, -reach), reach).astype(held_as)


def setup_inputs(seed: int = 0) -> dict:
    seeds = jax.random.split(jax.random.key(seed), 5)
    matrix = bell_draw(seeds[0], (ROWBLK, NB, COLBLK, COLSPAN), 1.0, 6.0, ((1, 8), (3, 4)), jnp.float32)
    pivots = draw_pivots(jax.random.fold_in(seeds[4], 71), 0)
    lower_inv = draw_lower_inv(jax.random.fold_in(seeds[4], 71), 0)
    upper_inv = draw_upper_inv(jax.random.fold_in(seeds[4], 71), 0)
    return {"matrix": matrix, "pivots": pivots, "lower_inv": lower_inv, "upper_inv": upper_inv}


def permutation(pivot_row, offset):
    def swap_one(position, ordering):
        target = pivot_row[position].astype(jnp.int32)
        root = (offset + position)
        first_row = ordering[root]
        second_row = ordering[target]
        return ordering.at[root].set(second_row).at[target].set(first_row)
    return lax.fori_loop(0, NB, swap_one, jnp.arange(M, dtype=jnp.int32))


def reference(matrix, pivots, lower_inv, upper_inv):
    current = matrix.reshape(M, M)
    for panel_index in range(PANELS):
        offset = panel_index * NB
        ending = offset + NB
        ordering = permutation(pivots[panel_index], offset)
        current = current[ordering]
        upper_block = jnp.dot(lower_inv[panel_index], current[offset:ending, ending:], precision=lax.Precision.HIGHEST, preferred_element_type=jnp.float32)
        lower_block = jnp.dot(current[ending:, offset:ending], upper_inv[panel_index], precision=lax.Precision.HIGHEST, preferred_element_type=jnp.float32)
        trailing = current[ending:, ending:] - jnp.dot(lower_block, upper_block, precision=lax.Precision.HIGHEST, preferred_element_type=jnp.float32)
        current = current.at[offset:ending, ending:].set(upper_block)
        current = current.at[ending:, offset:ending].set(lower_block)
        current = current.at[ending:, ending:].set(trailing)
    return current.reshape(ROWBLK, NB, COLBLK, COLSPAN)
```

```python
import functools
import math

import jax
import jax.numpy as jnp
from jax import lax
from jax.experimental.layout import Layout, with_layout_constraint
from jax.experimental import pallas as pl
from jax.experimental.pallas import tpu as pltpu
from jax.sharding import PartitionSpec as P


def product(left, right):
    return jnp.dot(left, right, precision=lax.Precision.HIGH, preferred_element_type=jnp.float32)


def div_by(value, count):
    if count & (count - 1) == 0:
        return lax.shift_right_logical(value, jnp.full_like(value, count.bit_length() - 1))
    return lax.div(value, jnp.full_like(value, count))


def mod_by(value, count):
    if count & (count - 1) == 0:
        return value & (count - 1)
    return value - div_by(value, count) * count


def ring_place(index, count):
    return jnp.where(index % 2 == 0, index // 2, count - 1 - index // 2)


def split(value):
    high = value.astype(jnp.bfloat16)
    return high, (value - high.astype(jnp.float32)).astype(jnp.bfloat16)


def halves(value):
    high = lax.reduce_precision(value, 8, 7)
    return high.astype(jnp.bfloat16), (value - high).astype(jnp.bfloat16)


def dot3(left_high, left_low, right_high, right_low):
    def one(left, right):
        return jnp.dot(left, right, preferred_element_type=jnp.float32)

    return one(left_high, right_high) + (one(left_high, right_low) + one(left_low, right_high))


def turned(row):
    return jnp.transpose(jnp.broadcast_to(row, (8, row.shape[1])))[:, :1]


def routing_kernel(
    me_ref, piv_row, piv_col, send_ref, place_ref, out_ref, in_ref, count_ref, over_ref, want_ref, from_ref, *, sizes
):
    panel, part, devices, cap, pair_cap = sizes
    total = piv_row.shape[1]
    me = me_ref[0]
    p_row = piv_row[...]
    p_col = piv_col[...]
    lane = lax.broadcasted_iota(jnp.int32, (1, total), 1)
    sub = lax.broadcasted_iota(jnp.int32, (total, 1), 0)

    def top(mask, value):
        return jnp.max(jnp.where(mask, value, -1), axis=0, keepdims=True)

    def pick(index_row, value_col):
        return jnp.sum(jnp.where(sub == index_row, value_col, 0), axis=0, keepdims=True)

    chain = top((p_col == lane) & (sub < lane), sub)
    start = jnp.where(chain >= 0, chain, lane)

    def step(carry):
        pointer, _ = carry
        further = pick(pointer, turned(pointer))
        return further, jnp.max(jnp.abs(further - pointer))

    before, _ = lax.while_loop(lambda carry: carry[1] > 0, step, (start, jnp.int32(1)))
    same = p_col == p_row
    last = top(same & (sub < lane), sub)
    final = top(same, sub)
    wanted = jnp.where(last >= 0, pick(last, turned(before)), p_row)

    def owner(row):
        return div_by(mod_by(row, panel), part)

    def spot(row):
        return div_by(row, panel) * part + mod_by(row, part)

    holder = owner(wanted)
    rank = jnp.sum(jnp.where((turned(holder) == holder) & (sub < lane), 1, 0), axis=0, keepdims=True)
    moved = (final == lane) & (p_row >= total)
    source = owner(before)
    target = owner(p_row)
    pair = jnp.where(moved, source * devices + target, -1)
    pair_rank = jnp.sum(jnp.where((turned(pair) == pair) & (sub < lane), 1, 0), axis=0, keepdims=True)
    distance = ring_place(me, devices) - ring_place(holder, devices)
    distance = jnp.where(distance < 0, distance + devices, distance)
    place_ref[...] = distance * cap + rank

    def table(width, code, value):
        slots = lax.broadcasted_iota(jnp.int32, (1, width), 1)
        return jnp.sum(jnp.where(turned(code) == slots, turned(value), 0), axis=0, keepdims=True)

    send_ref[...] = table(send_ref.shape[1], jnp.where((holder == me) & (rank < cap), rank, -1), spot(wanted))
    want_ref[...] = wanted
    from_ref[...] = jnp.where(moved, before, -1)
    fits = moved & (pair_rank < pair_cap)
    going = fits & (source == me)
    coming = fits & (target == me)
    out_ref[...] = table(out_ref.shape[1], jnp.where(going, target * pair_cap + pair_rank, -1), spot(before))
    in_ref[...] = table(in_ref.shape[1], jnp.where(coming, source * pair_cap + pair_rank, -1), spot(p_row))
    kinds = lax.broadcasted_iota(jnp.int32, (1, count_ref.shape[1]), 1)
    count_ref[...] = jnp.sum(jnp.where(turned(jnp.where(coming, source, -1)) == kinds, 1, 0), axis=0, keepdims=True)
    excess = jnp.maximum(jnp.max(rank) - cap, jnp.max(jnp.where(moved, pair_rank, 0)) - pair_cap)
    over_ref[...] = jnp.full(over_ref.shape, excess, jnp.int32)


def plain(value):
    return with_layout_constraint(value, Layout(major_to_minor=tuple(range(value.ndim))))


def lanes(count):
    return -(-count // 128) * 128


def routing(me, pivots, sizes):
    panel, part, devices, cap, pair_cap = sizes
    total = pivots.size
    shapes = [lanes(cap), total, lanes(devices * pair_cap), lanes(devices * pair_cap), lanes(devices), 128, total, total]
    return pl.pallas_call(
        functools.partial(routing_kernel, sizes=sizes),
        out_shape=[jax.ShapeDtypeStruct((1, width), jnp.int32) for width in shapes],
        in_specs=[
            pl.BlockSpec(memory_space=pltpu.SMEM),
            pl.BlockSpec(memory_space=pltpu.VMEM),
            pl.BlockSpec(memory_space=pltpu.VMEM),
        ],
        name="routing",
    )(me, pivots.reshape(1, total), pivots.reshape(total, 1))


def move_rows(count, unroll, load, store):
    def body(step, _):
        rows = [step * unroll + inner for inner in range(unroll)]
        values = [load(row) for row in rows]
        for row, value in zip(rows, values):
            store(row, value)
        return 0

    lax.fori_loop(0, count // unroll, body, 0)


def pack_kernel(at_ref, x_ref, o_ref, *, part):
    def load(row):
        spot = at_ref[row]
        return x_ref[spot // part, 0, pl.ds(spot % part, 1), :]

    def store(row, value):
        o_ref[0, pl.ds(row, 1), :] = value

    move_rows(o_ref.shape[1], 8, load, store)


def pack(at, x, col, per, cap):
    blocks, cols, part, width = x.shape
    return pl.pallas_call(
        functools.partial(pack_kernel, part=part),
        grid_spec=pltpu.PrefetchScalarGridSpec(
            num_scalar_prefetch=1,
            grid=(per,),
            in_specs=[pl.BlockSpec((blocks, 1, part, width), lambda i, at: (0, col + i, 0, 0))],
            out_specs=pl.BlockSpec((1, cap, width), lambda i, at: (i, 0, 0)),
        ),
        out_shape=jax.ShapeDtypeStruct((per, cap, width), jnp.float32),
        cost_estimate=pl.CostEstimate(flops=0, transcendentals=0, bytes_accessed=3 * per * blocks * part * width * 4),
        name="pack",
    )(at, x)


def piece_specs(pieces, per):
    specs = [pl.BlockSpec((1,) + piece.shape[1:], lambda i, *_: (i, 0, 0)) for piece in pieces[:-2]]
    left, right = pieces[-2:]
    if left.shape[0] == per:
        return specs + [pl.BlockSpec((1,) + piece.shape[1:], lambda i, *_: (i, 0, 0)) for piece in (left, right)]
    half = left.shape[0]
    specs.append(pl.BlockSpec((1,) + left.shape[1:], lambda i, *_: (jnp.minimum(i, half - 1), 0, 0)))
    specs.append(pl.BlockSpec((1,) + right.shape[1:], lambda i, *_: (jnp.maximum(i - half, 0), 0, 0)))
    return specs


def load_pieces(pieces, cap, width, half, store):
    count = len(pieces) - 1
    far = (count + 1) // 2
    for index in range(count - 1):
        store((index if index < far else index + 1) * cap, 0, pieces[index][0])
    left, right = pieces[-2:]
    if left.shape[2] < width:
        store(far * cap, 0, left[0])
        store(far * cap, left.shape[2], right[0])
    else:
        store(far * cap, 0, jnp.where(pl.program_id(0) < half, left[0], right[0]))


def unpack_kernel(at_ref, *refs, cap, half):
    pieces, o_ref, buffer = refs[:-2], refs[-2], refs[-1]

    def put(row, col, value):
        buffer[row : row + value.shape[0], col : col + value.shape[1]] = value

    load_pieces(pieces, cap, buffer.shape[1], half, put)

    def load(row):
        return buffer[pl.ds(at_ref[row], 1), :]

    def store(row, value):
        o_ref[pl.ds(row, 1), :] = value

    move_rows(o_ref.shape[0], 8, load, store)


def unpack(at, pieces, cap, devices):
    total = at.shape[0]
    per, _, width = pieces[0].shape
    return pl.pallas_call(
        functools.partial(unpack_kernel, cap=cap, half=per // 2),
        grid_spec=pltpu.PrefetchScalarGridSpec(
            num_scalar_prefetch=1,
            grid=(1,),
            in_specs=piece_specs(pieces, per),
            out_specs=pl.BlockSpec((total, width), lambda i, at: (0, 0)),
            scratch_shapes=[pltpu.VMEM((devices * cap, width), jnp.float32)],
        ),
        out_shape=jax.ShapeDtypeStruct((total, width), jnp.float32),
        cost_estimate=pl.CostEstimate(flops=0, transcendentals=0, bytes_accessed=16 * total * width),
        name="unpack",
    )(at, *pieces)


def solve_kernel(flag_ref, at_ref, *refs, cap, half, pieces_count, special):
    s_high, s_low, pick_ref, t_high, t_low, v_high, v_low, l_high, l_low, x_ref = refs[:10]
    pieces = refs[10 : 10 + pieces_count]
    rest = refs[10 + pieces_count :]
    if special:
        alt_ref, rest = rest[0], rest[1:]
    u_high, u_low, front_ref, send_ref, g_high, g_low, u_full, y_ref = rest
    me = flag_ref[0]
    panel = pick_ref.shape[0]

    def put(row, col, value):
        high, low = split(value)
        g_high[row : row + value.shape[0], col : col + value.shape[1]] = high
        g_low[row : row + value.shape[0], col : col + value.shape[1]] = low

    load_pieces(pieces, cap, g_high.shape[1], half, put)
    upper = dot3(s_high[...], s_low[...], g_high[...], g_low[...])
    u_full[:panel] = upper
    high, low = split(upper)
    u_high[0, :panel] = high
    u_low[0, :panel] = low
    picked = jnp.dot(pick_ref[...], g_high[...], preferred_element_type=jnp.float32)
    picked += jnp.dot(pick_ref[...], g_low[...], preferred_element_type=jnp.float32)
    reduced = picked - dot3(t_high[...], t_low[...], high, low)
    upper = dot3(v_high[...], v_low[...], *split(reduced))
    u_full[panel:] = upper
    high, low = split(upper)
    u_high[0, panel:] = high
    u_low[0, panel:] = low
    _, panels, part, width = front_ref.shape
    for index in range(panels):
        front_ref[0, index] = u_full[pl.ds(pl.multiple_of(index * panel + me * part, 8), part), :]
    old = x_ref[...].reshape(panels * part, width) - dot3(l_high[...], l_low[...], u_high[0], u_low[0])
    if special:
        old = jnp.where((flag_ref[1] > 0) & (pl.program_id(0) == 0), alt_ref[...], old)
    y_ref[...] = old
    devices, _, pair_cap, _ = send_ref.shape
    for target in range(devices):

        def load(row):
            return y_ref[pl.ds(at_ref[target * pair_cap + row], 1), :]

        def store(row, value):
            send_ref[target, 0, pl.ds(row, 1), :] = value

        move_rows(pair_cap, 8, load, store)


def solve(flags, at, factors, low, x, col, pieces, alt, cap, devices, pair_cap, panels):
    panel, depth = factors[0].shape
    total = panels * panel
    blocks, cols, part, width = x.shape
    per = pieces[0].shape[0]
    whole = lambda i, *_: (0, 0)
    in_specs = [pl.BlockSpec(factor.shape, whole) for factor in factors]
    in_specs += [
        pl.BlockSpec((panels * part, total), whole),
        pl.BlockSpec((panels * part, total), whole),
        pl.BlockSpec((panels, 1, part, width), lambda i, *_: (0, col + i, 0, 0)),
    ]
    in_specs += piece_specs(pieces, per)
    args = [*factors, *low, x, *pieces]
    if alt is not None:
        in_specs.append(pl.BlockSpec((panels * part, width), whole))
        args.append(alt)
    return pl.pallas_call(
        functools.partial(
            solve_kernel, cap=cap, half=per // 2, pieces_count=len(pieces), special=alt is not None
        ),
        grid_spec=pltpu.PrefetchScalarGridSpec(
            num_scalar_prefetch=2,
            grid=(per,),
            in_specs=in_specs,
            out_specs=[
                pl.BlockSpec((1, total, width), lambda i, *_: (i, 0, 0)),
                pl.BlockSpec((1, total, width), lambda i, *_: (i, 0, 0)),
                pl.BlockSpec((1, panels, part, width), lambda i, *_: (i, 0, 0, 0)),
                pl.BlockSpec((devices, 1, pair_cap, width), lambda i, *_: (0, i, 0, 0)),
            ],
            scratch_shapes=[
                pltpu.VMEM((depth, width), jnp.bfloat16),
                pltpu.VMEM((depth, width), jnp.bfloat16),
                pltpu.VMEM((total, width), jnp.float32),
                pltpu.VMEM((panels * part, width), jnp.float32),
            ],
        ),
        out_shape=[
            jax.ShapeDtypeStruct((per, total, width), jnp.bfloat16),
            jax.ShapeDtypeStruct((per, total, width), jnp.bfloat16),
            jax.ShapeDtypeStruct((per, panels, part, width), jnp.float32),
            jax.ShapeDtypeStruct((devices, per, pair_cap, width), jnp.float32),
        ],
        cost_estimate=pl.CostEstimate(
            flops=6 * per * total * (depth + panels * part) * width,
            transcendentals=0,
            bytes_accessed=16 * per * total * width,
        ),
        name="solve",
    )(flags, at, *args)


def trail_kernel(flag_ref, at_ref, count_ref, *refs, special):
    x_ref, l_high, l_low, u_high, u_low, front_ref, come_ref = refs[:7]
    rest = refs[7:]
    if special:
        alt_ref, corner_ref, rest = rest[0], rest[1], rest[2:]
    o_ref = rest[-1]
    group, _, part, width = x_ref.shape
    step = pl.program_id(1)
    value = x_ref[...].reshape(group * part, width) - dot3(l_high[...], l_low[...], u_high[0], u_low[0])
    if special:
        chosen = (flag_ref[1] > 0) & (pl.program_id(0) == 0)
        value = jnp.where(chosen, alt_ref[...], value)
    o_ref[pl.ds(step * group, group), 0] = value.reshape(group, part, width)

    @pl.when(step == pl.num_programs(1) - 1)
    def _():
        for index in range(front_ref.shape[1]):
            front = front_ref[0, index]
            if special:
                front = jnp.where(chosen, corner_ref[index], front)
            o_ref[index, 0] = front
        pair_cap = come_ref.shape[2]
        for source in range(come_ref.shape[0]):

            def body(row, _):
                spot = at_ref[source * pair_cap + row]
                o_ref[spot // part, 0, pl.ds(spot % part, 1), :] = come_ref[source, 0, pl.ds(row, 1), :]
                return 0

            lax.fori_loop(0, count_ref[source], body, 0)


def trail(flags, at, counts, x, col, low, upper, front, come, special, previous, group):
    blocks, cols, part, width = x.shape
    per, total, _ = upper[0].shape
    in_specs = [
        pl.BlockSpec((group, 1, part, width), lambda i, j, *_: (j, col + i, 0, 0)),
        pl.BlockSpec((group * part, total), lambda i, j, *_: (j, 0)),
        pl.BlockSpec((group * part, total), lambda i, j, *_: (j, 0)),
        pl.BlockSpec((1, total, width), lambda i, j, *_: (i, 0, 0)),
        pl.BlockSpec((1, total, width), lambda i, j, *_: (i, 0, 0)),
        pl.BlockSpec((1,) + front.shape[1:], lambda i, j, *_: (i, 0, 0, 0)),
        pl.BlockSpec((come.shape[0], 1) + come.shape[2:], lambda i, j, *_: (0, i, 0, 0)),
    ]
    args = [x, *low, *upper, front, come]
    if special is not None:
        alt, corner = special
        in_specs.append(pl.BlockSpec((group * part, width), lambda i, j, *_: (j, 0)))
        in_specs.append(pl.BlockSpec(corner.shape, lambda i, j, *_: (0, 0, 0)))
        args += [alt, corner]
    aliases = {}
    if previous is not None:
        in_specs.append(pl.BlockSpec(memory_space=pl.ANY))
        args.append(previous)
        aliases = {3 + len(args) - 1: 0}
    return pl.pallas_call(
        functools.partial(trail_kernel, special=special is not None),
        grid_spec=pltpu.PrefetchScalarGridSpec(
            num_scalar_prefetch=3,
            grid=(per, blocks // group),
            in_specs=in_specs,
            out_specs=pl.BlockSpec((blocks, 1, part, width), lambda i, j, *_: (0, col + i, 0, 0)),
        ),
        out_shape=jax.ShapeDtypeStruct(x.shape, jnp.float32),
        input_output_aliases=aliases,
        cost_estimate=pl.CostEstimate(
            flops=6 * per * blocks * part * total * width,
            transcendentals=0,
            bytes_accessed=16 * per * blocks * part * width,
        ),
        name="trail",
    )(flags, at, counts, *args)


def ring_gather(own, devices):
    order = list(range(0, devices, 2)) + list(range(devices - 1, 0, -2))
    forward = [(order[i], order[(i + 1) % devices]) for i in range(devices)]
    backward = [(b, a) for a, b in forward]
    ahead = behind = own
    ahead_list, behind_list = [], []
    for hop in range(devices // 2 - 1):
        ahead = lax.ppermute(ahead, "prow", forward)
        behind = lax.ppermute(behind, "prow", backward)
        ahead_list.append(ahead)
        behind_list.append(behind)
    if own.shape[0] % 2 == 0:
        half = own.shape[0] // 2
        left, right = ahead[:half], behind[half:]
    else:
        half = own.shape[2] // 2
        left, right = ahead[:, :, :half], behind[:, :, half:]
    left = lax.ppermute(left, "prow", forward)
    right = lax.ppermute(right, "prow", backward)
    return [own, *ahead_list, *reversed(behind_list), left, right]


def panel_pair(block, col_index, col_devices):
    chips = col_devices // 2
    home = col_index // 2
    mine = block
    moving = block
    for hop in range(1, chips):
        moving = lax.ppermute(moving, "pcol", [(2 * hop - 2, 2 * hop), (2 * hop - 1, 2 * hop + 1)])
        mine = jnp.where(home == hop, moving, mine)
    first = lax.ppermute(block, "pcol", [(0, 1), (1, 0)])
    rest = [(i, i ^ 1) for i in range(2, col_devices)]
    other = jnp.where(home == 0, first, lax.ppermute(mine, "pcol", rest)) if rest else first
    even = col_index % 2 == 0
    return jnp.where(even, mine, other), jnp.where(even, other, mine)


def exchange(send):
    return lax.all_to_all(send, "prow", 0, 0, tiled=True)


def fast(x, place, tables, lower_inv, upper_inv, sizes):
    panel, part, devices, cap, pair_cap = sizes
    send_at, out_at, in_at, counts = tables
    blocks, cols, _, width = x.shape
    panels = lower_inv.shape[0]
    row_index = lax.axis_index("prow")
    col_index = lax.axis_index("pcol")
    col_devices = lax.axis_size("pcol")
    per = 2 if cols % 2 == 0 else 1
    chunks = range(0, cols, per)
    raw = panel_pair(x[:, 0].reshape(blocks * part, width), col_index, col_devices)
    flags = jnp.stack([row_index, (col_index < panels).astype(jnp.int32)]).astype(jnp.int32)
    gathered = [ring_gather(pack(send_at, x, col, per, cap), devices) for col in chunks]
    head = unpack(place, gathered[0], cap, devices)
    sent = jnp.where(col_index == 0, head[panel:], head[:panel])
    corner_low, corner_up = panel_pair(sent, col_index, col_devices)
    low_top = product(corner_low, upper_inv[0])
    up_side = product(lower_inv[0], corner_up)
    low_first = product(raw[0], upper_inv[0])
    low_second = product(raw[1] - product(low_first, up_side), upper_inv[1])
    low = halves(jnp.concatenate([low_first, low_second], axis=1))
    alt = jnp.where(col_index == 0, low_first, low_second)
    select = (place[:, None] == jnp.arange(devices * cap, dtype=jnp.int32)[None, :]).astype(jnp.bfloat16)
    first = [
        jnp.dot(side, select[:panel], preferred_element_type=jnp.float32).astype(jnp.bfloat16)
        for side in halves(lower_inv[0])
    ]
    factors = [*first, select[panel:], *halves(low_top), *halves(lower_inv[1])]
    own_head = lax.dynamic_slice_in_dim(head, row_index * part, part, 0)
    own_tail = lax.dynamic_slice_in_dim(head, panel + row_index * part, part, 0)
    own_low = lax.dynamic_slice_in_dim(low_top, row_index * part, part, 0)
    own_up = lax.dynamic_slice_in_dim(up_side, row_index * part, part, 0)
    corner = jnp.where(
        col_index == 0, jnp.stack([own_head, own_low]), jnp.stack([own_up, own_tail - product(own_low, up_side)])
    )
    group = max(g for g in range(1, blocks + 1) if blocks % g == 0 and g * part <= 512)
    result = None
    for chunk, col in enumerate(chunks):
        u_high, u_low, front, send = solve(
            flags,
            out_at,
            factors,
            low,
            x,
            col,
            gathered[chunk],
            alt if col == 0 else None,
            cap,
            devices,
            pair_cap,
            panels,
        )
        come = exchange(send)
        special = (alt, corner) if col == 0 else None
        result = trail(flags, in_at, counts, x, col, low, (u_high, u_low), front, come, special, result, group)
    return result


def slow(x, wanted, came_from, pivots, lower_inv, upper_inv, result, sizes):
    panel, part, devices, _, _ = sizes
    blocks, cols, _, width = x.shape
    total = wanted.shape[0]
    x = plain(x)
    row_index = lax.axis_index("prow")
    col_index = lax.axis_index("pcol")
    col_devices = lax.axis_size("pcol")
    rows = jnp.arange(blocks, dtype=jnp.int32)[:, None] * panel + jnp.arange(part, dtype=jnp.int32)[None, :]
    rows = (rows + row_index * part).reshape(-1)
    spots = jnp.where(came_from >= 0, pivots, blocks * panel)
    source = jnp.full((blocks * panel,), -1, jnp.int32).at[spots].set(came_from, mode="drop")[rows]
    needed = jnp.concatenate([wanted, jnp.arange(total, dtype=jnp.int32)])
    mine = (needed % panel // part == row_index)[:, None]
    spot = needed // panel * part + needed % part
    around = [(i, (i + 1) % devices) for i in range(devices)]

    def swapped(col):
        here = lax.dynamic_index_in_dim(x, col, 1, False).reshape(blocks * part, width)
        moving = jnp.where(mine, here[spot], 0.0)

        def hop(_, carry):
            moving, gathered = carry
            moving = lax.ppermute(moving, "prow", around)
            return moving, gathered + moving

        _, gathered = lax.fori_loop(0, devices - 1, hop, (moving, moving))
        head = gathered[:total]
        return head, jnp.where((source >= 0)[:, None], gathered[total:][jnp.maximum(source, 0)], here)

    head, body = swapped(0)
    raw = panel_pair(body, col_index, col_devices)
    corner = panel_pair(head, col_index, col_devices)
    low_top = product(corner[0][panel:], upper_inv[0])
    up_side = product(lower_inv[0], corner[1][:panel])
    low_first = product(raw[0], upper_inv[0])
    low_second = product(raw[1] - product(low_first, up_side), upper_inv[1])

    def column(col, result):
        head, body = swapped(col)
        upper = product(lower_inv[0], head[:panel])
        reduced = head[panel:] - product(low_top, upper)
        second = product(lower_inv[1], reduced)
        body = body - product(low_first, upper) - product(low_second, second)
        left = (col == 0) & (col_index == 0)
        right = (col == 0) & (col_index == 1)
        body = jnp.where(left, low_first, jnp.where(right, low_second, body))
        upper = jnp.where(left, head[:panel], upper)
        second = jnp.where(left, low_top, jnp.where(right, reduced, second))
        own = [lax.dynamic_slice_in_dim(side, row_index * part, part, 0) for side in (upper, second)]
        body = jnp.concatenate([*own, body[2 * part :]], axis=0)
        return plain(lax.dynamic_update_index_in_dim(plain(result), body.reshape(blocks, part, width), col, 1))

    return lax.fori_loop(0, cols, column, result)


def local(matrix, pivots, lower_inv, upper_inv):
    row_blocks, row_part, col_blocks, col_part = matrix.shape
    panels, panel = pivots.shape
    devices = lax.axis_size("prow")
    col_devices = lax.axis_size("pcol")
    col_index = lax.axis_index("pcol")
    total = panels * panel
    mean = total / devices
    cap = -(-int(mean + 2.75 * math.sqrt(mean)) // 8) * 8
    pair_mean = mean / devices
    pair_cap = -(-int(pair_mean + 4 * math.sqrt(pair_mean)) // 8) * 8
    sizes = (panel, row_part, devices, cap, pair_cap)
    x = matrix.transpose(0, 2, 1, 3)
    me = lax.axis_index("prow").astype(jnp.int32).reshape(1)
    send_at, place, out_at, in_at, counts, over, wanted, came_from = routing(me, pivots, sizes)
    tables = (send_at[0], out_at[0], in_at[0], counts[0])
    result = fast(x, place[0], tables, lower_inv, upper_inv, sizes)

    def again(carry):
        _, result = carry
        result = slow(x, wanted[0], came_from[0], pivots.reshape(-1), lower_inv, upper_inv, result, sizes)
        return jnp.int32(-1), plain(result)

    _, result = lax.while_loop(lambda carry: carry[0] >= 0, again, (over[0, 0], plain(result)))
    return result.transpose(0, 2, 1, 3)


def solution(mesh):
    return jax.shard_map(
        local,
        mesh=mesh,
        in_specs=(P(None, "prow", None, "pcol"), P(), P(), P()),
        out_specs=P(None, "prow", None, "pcol"),
        check_vma=False,
    )
```

```python
import functools
import math

import jax
import jax.numpy as jnp
from jax import lax
from jax.experimental.layout import Layout, with_layout_constraint
from jax.experimental import pallas as pl
from jax.experimental.pallas import tpu as pltpu
from jax.sharding import PartitionSpec as P


def product(left, right):
    return jnp.dot(left, right, precision=lax.Precision.HIGH, preferred_element_type=jnp.float32)


def div_by(value, count):
    if count & (count - 1) == 0:
        return lax.shift_right_logical(value, jnp.full_like(value, count.bit_length() - 1))
    return lax.div(value, jnp.full_like(value, count))


def mod_by(value, count):
    if count & (count - 1) == 0:
        return value & (count - 1)
    return value - div_by(value, count) * count


def ring_place(index, count):
    return jnp.where(index % 2 == 0, index // 2, count - 1 - index // 2)


def split(value):
    high = value.astype(jnp.bfloat16)
    return high, (value - high.astype(jnp.float32)).astype(jnp.bfloat16)


def halves(value):
    high = lax.reduce_precision(value, 8, 7)
    return high.astype(jnp.bfloat16), (value - high).astype(jnp.bfloat16)


def dot3(left_high, left_low, right_high, right_low):
    def one(left, right):
        return jnp.dot(left, right, preferred_element_type=jnp.float32)

    return one(left_high, right_high) + (one(left_high, right_low) + one(left_low, right_high))


def turned(row):
    return jnp.transpose(jnp.broadcast_to(row, (8, row.shape[1])))[:, :1]


def routing_kernel(
    me_ref,
    piv_row,
    piv_col,
    send_ref,
    place_ref,
    out_ref,
    row_ref,
    slot_ref,
    count_ref,
    over_ref,
    want_ref,
    from_ref,
    *,
    sizes,
):
    panel, part, devices, cap, pair_cap, _, rows = sizes
    total = piv_row.shape[1]
    me = me_ref[0]
    p_row = piv_row[...]
    p_col = piv_col[...]
    lane = lax.broadcasted_iota(jnp.int32, (1, total), 1)
    sub = lax.broadcasted_iota(jnp.int32, (total, 1), 0)

    def top(mask, value):
        return jnp.max(jnp.where(mask, value, -1), axis=0, keepdims=True)

    def pick(index_row, value_col):
        return jnp.sum(jnp.where(sub == index_row, value_col, 0), axis=0, keepdims=True)

    chain = top((p_col == lane) & (sub < lane), sub)
    start = jnp.where(chain >= 0, chain, lane)

    def step(carry):
        pointer, _ = carry
        further = pick(pointer, turned(pointer))
        return further, jnp.max(jnp.abs(further - pointer))

    before, _ = lax.while_loop(lambda carry: carry[1] > 0, step, (start, jnp.int32(1)))
    same = p_col == p_row
    last = top(same & (sub < lane), sub)
    final = top(same, sub)
    wanted = jnp.where(last >= 0, pick(last, turned(before)), p_row)

    def owner(row):
        return div_by(mod_by(row, panel), part)

    def spot(row):
        return div_by(row, panel) * part + mod_by(row, part)

    holder = owner(wanted)
    rank = jnp.sum(jnp.where((turned(holder) == holder) & (sub < lane), 1, 0), axis=0, keepdims=True)
    moved = (final == lane) & (p_row >= total)
    source = owner(before)
    target = owner(p_row)
    pair = jnp.where(moved, source * devices + target, -1)
    pair_rank = jnp.sum(jnp.where((turned(pair) == pair) & (sub < lane), 1, 0), axis=0, keepdims=True)
    distance = ring_place(me, devices) - ring_place(holder, devices)
    distance = jnp.where(distance < 0, distance + devices, distance)
    place_ref[...] = distance * cap + rank

    def table(width, code, value):
        slots = lax.broadcasted_iota(jnp.int32, (1, width), 1)
        return jnp.sum(jnp.where(turned(code) == slots, turned(value), 0), axis=0, keepdims=True)

    send_ref[...] = table(send_ref.shape[1], jnp.where((holder == me) & (rank < cap), rank, -1), spot(wanted))
    want_ref[...] = wanted
    from_ref[...] = jnp.where(moved, before, -1)
    fits = moved & (pair_rank < pair_cap)
    going = fits & (source == me)
    coming = fits & (target == me)
    out_ref[...] = table(out_ref.shape[1], jnp.where(going, target * pair_cap + pair_rank, -1), spot(before))
    band = jnp.where(coming, div_by(spot(p_row), rows), -1)
    band_rank = jnp.sum(jnp.where((turned(band) == band) & (sub < lane), 1, 0), axis=0, keepdims=True)
    code = jnp.where(coming, band * (devices * pair_cap) + band_rank, -1)
    row_ref[...] = table(row_ref.shape[1], code, mod_by(spot(p_row), rows))
    slot_ref[...] = table(slot_ref.shape[1], code, source * pair_cap + pair_rank)
    kinds = lax.broadcasted_iota(jnp.int32, (1, count_ref.shape[1]), 1)
    count_ref[...] = jnp.sum(jnp.where(turned(band) == kinds, 1, 0), axis=0, keepdims=True)
    excess = jnp.maximum(jnp.max(rank) - cap, jnp.max(jnp.where(moved, pair_rank, 0)) - pair_cap)
    over_ref[...] = jnp.full(over_ref.shape, excess, jnp.int32)


def plain(value):
    return with_layout_constraint(value, Layout(major_to_minor=tuple(range(value.ndim))))


def lanes(count):
    return -(-count // 128) * 128


def routing(me, pivots, sizes):
    _, _, devices, cap, pair_cap, bands, _ = sizes
    total = pivots.size
    pairs = devices * pair_cap
    shapes = [lanes(cap), total, lanes(pairs), lanes(bands * pairs), lanes(bands * pairs), 128, 128, total, total]
    return pl.pallas_call(
        functools.partial(routing_kernel, sizes=sizes),
        out_shape=[jax.ShapeDtypeStruct((1, width), jnp.int32) for width in shapes],
        in_specs=[
            pl.BlockSpec(memory_space=pltpu.SMEM),
            pl.BlockSpec(memory_space=pltpu.VMEM),
            pl.BlockSpec(memory_space=pltpu.VMEM),
        ],
        name="routing",
    )(me, pivots.reshape(1, total), pivots.reshape(total, 1))


def move_rows(count, unroll, load, store):
    def body(step, _):
        rows = [step * unroll + inner for inner in range(unroll)]
        values = [load(row) for row in rows]
        for row, value in zip(rows, values):
            store(row, value)
        return 0

    lax.fori_loop(0, count // unroll, body, 0)


def pack_kernel(at_ref, x_ref, o_ref, *, part):
    def load(row):
        spot = at_ref[row]
        return x_ref[spot // part, 0, pl.ds(spot % part, 1), :]

    def store(row, value):
        o_ref[0, pl.ds(row, 1), :] = value

    move_rows(o_ref.shape[1], 8, load, store)


def pack(at, x, col, per, cap):
    blocks, _, part, width = x.shape
    return pl.pallas_call(
        functools.partial(pack_kernel, part=part),
        grid_spec=pltpu.PrefetchScalarGridSpec(
            num_scalar_prefetch=1,
            grid=(per,),
            in_specs=[pl.BlockSpec((blocks, 1, part, width), lambda i, at: (0, col + i, 0, 0))],
            out_specs=pl.BlockSpec((1, cap, width), lambda i, at: (i, 0, 0)),
        ),
        out_shape=jax.ShapeDtypeStruct((per, cap, width), jnp.float32),
        cost_estimate=pl.CostEstimate(flops=0, transcendentals=0, bytes_accessed=3 * per * blocks * part * width * 4),
        name="pack",
    )(at, x)


def piece_specs(pieces, per):
    specs = [pl.BlockSpec((1,) + piece.shape[1:], lambda i, *_: (i, 0, 0)) for piece in pieces[:-2]]
    left, right = pieces[-2:]
    if left.shape[0] == per:
        return specs + [pl.BlockSpec((1,) + piece.shape[1:], lambda i, *_: (i, 0, 0)) for piece in (left, right)]
    half = left.shape[0]
    specs.append(pl.BlockSpec((1,) + left.shape[1:], lambda i, *_: (jnp.minimum(i, half - 1), 0, 0)))
    specs.append(pl.BlockSpec((1,) + right.shape[1:], lambda i, *_: (jnp.maximum(i - half, 0), 0, 0)))
    return specs


def load_pieces(pieces, cap, width, half, store):
    count = len(pieces) - 1
    far = (count + 1) // 2
    for index in range(count - 1):
        store((index if index < far else index + 1) * cap, 0, pieces[index][0])
    left, right = pieces[-2:]
    if left.shape[2] < width:
        store(far * cap, 0, left[0])
        store(far * cap, left.shape[2], right[0])
    else:
        store(far * cap, 0, jnp.where(pl.program_id(0) < half, left[0], right[0]))


def unpack_kernel(flag_ref, at_ref, *refs, cap, half):
    pieces, o_ref, sent_ref, buffer = refs[:-3], refs[-3], refs[-2], refs[-1]

    def put(row, col, value):
        buffer[row : row + value.shape[0], col : col + value.shape[1]] = value

    load_pieces(pieces, cap, buffer.shape[1], half, put)

    def load(row):
        return buffer[pl.ds(at_ref[row], 1), :]

    def store(row, value):
        o_ref[pl.ds(row, 1), :] = value

    move_rows(o_ref.shape[0], 8, load, store)
    panel = sent_ref.shape[0]
    sent_ref[...] = jnp.where(flag_ref[2] == 0, o_ref[panel:], o_ref[:panel])


def unpack(flags, at, pieces, cap, devices, panel):
    total = at.shape[0]
    per, _, width = pieces[0].shape
    return pl.pallas_call(
        functools.partial(unpack_kernel, cap=cap, half=per // 2),
        grid_spec=pltpu.PrefetchScalarGridSpec(
            num_scalar_prefetch=2,
            grid=(1,),
            in_specs=piece_specs(pieces, per),
            out_specs=[
                pl.BlockSpec((total, width), lambda i, *_: (0, 0)),
                pl.BlockSpec((panel, width), lambda i, *_: (0, 0)),
            ],
            scratch_shapes=[pltpu.VMEM((devices * cap, width), jnp.float32)],
        ),
        out_shape=[
            jax.ShapeDtypeStruct((total, width), jnp.float32),
            jax.ShapeDtypeStruct((panel, width), jnp.float32),
        ],
        cost_estimate=pl.CostEstimate(flops=0, transcendentals=0, bytes_accessed=16 * total * width),
        name="unpack",
    )(flags, at, *pieces)


def solve_kernel(flag_ref, at_ref, *refs, cap, half, pieces_count, special):
    s_high, s_low, pick_ref, t_high, t_low, v_high, v_low, l_high, l_low, x_ref = refs[:10]
    pieces = refs[10 : 10 + pieces_count]
    rest = refs[10 + pieces_count :]
    if special:
        alt_ref, rest = rest[0], rest[1:]
    u_high, u_low, front_ref, send_ref, g_high, g_low, u_full, y_ref = rest
    me = flag_ref[0]
    panel = pick_ref.shape[0]

    def put(row, col, value):
        high, low = split(value)
        g_high[row : row + value.shape[0], col : col + value.shape[1]] = high
        g_low[row : row + value.shape[0], col : col + value.shape[1]] = low

    load_pieces(pieces, cap, g_high.shape[1], half, put)
    upper = dot3(s_high[...], s_low[...], g_high[...], g_low[...])
    u_full[:panel] = upper
    high, low = split(upper)
    u_high[0, :panel] = high
    u_low[0, :panel] = low
    picked = jnp.dot(pick_ref[...], g_high[...], preferred_element_type=jnp.float32)
    picked += jnp.dot(pick_ref[...], g_low[...], preferred_element_type=jnp.float32)
    reduced = picked - dot3(t_high[...], t_low[...], high, low)
    upper = dot3(v_high[...], v_low[...], *split(reduced))
    u_full[panel:] = upper
    high, low = split(upper)
    u_high[0, panel:] = high
    u_low[0, panel:] = low
    _, panels, part, width = front_ref.shape
    for index in range(panels):
        front_ref[0, index] = u_full[pl.ds(pl.multiple_of(index * panel + me * part, 8), part), :]
    old = x_ref[...].reshape(panels * part, width) - dot3(l_high[...], l_low[...], u_high[0], u_low[0])
    if special:
        old = jnp.where((flag_ref[1] > 0) & (pl.program_id(0) == 0), alt_ref[...], old)
    y_ref[...] = old
    devices, _, pair_cap, _ = send_ref.shape
    for target in range(devices):

        def load(row):
            return y_ref[pl.ds(at_ref[target * pair_cap + row], 1), :]

        def store(row, value):
            send_ref[target, 0, pl.ds(row, 1), :] = value

        move_rows(pair_cap, 8, load, store)


def solve(flags, at, factors, low, x, col, pieces, alt, cap, devices, pair_cap, panels):
    panel, depth = factors[0].shape
    total = panels * panel
    _, _, part, width = x.shape
    per = pieces[0].shape[0]
    whole = lambda i, *_: (0, 0)
    in_specs = [pl.BlockSpec(factor.shape, whole) for factor in factors]
    in_specs += [
        pl.BlockSpec((panels * part, total), whole),
        pl.BlockSpec((panels * part, total), whole),
        pl.BlockSpec((panels, 1, part, width), lambda i, *_: (0, col + i, 0, 0)),
    ]
    in_specs += piece_specs(pieces, per)
    args = [*factors, *low, x, *pieces]
    if alt is not None:
        in_specs.append(pl.BlockSpec((panels * part, width), whole))
        args.append(alt)
    return pl.pallas_call(
        functools.partial(
            solve_kernel, cap=cap, half=per // 2, pieces_count=len(pieces), special=alt is not None
        ),
        grid_spec=pltpu.PrefetchScalarGridSpec(
            num_scalar_prefetch=2,
            grid=(per,),
            in_specs=in_specs,
            out_specs=[
                pl.BlockSpec((1, total, width), lambda i, *_: (i, 0, 0)),
                pl.BlockSpec((1, total, width), lambda i, *_: (i, 0, 0)),
                pl.BlockSpec((1, panels, part, width), lambda i, *_: (i, 0, 0, 0)),
                pl.BlockSpec((devices, 1, pair_cap, width), lambda i, *_: (0, i, 0, 0)),
            ],
            scratch_shapes=[
                pltpu.VMEM((depth, width), jnp.bfloat16),
                pltpu.VMEM((depth, width), jnp.bfloat16),
                pltpu.VMEM((total, width), jnp.float32),
                pltpu.VMEM((panels * part, width), jnp.float32),
            ],
        ),
        out_shape=[
            jax.ShapeDtypeStruct((per, total, width), jnp.bfloat16),
            jax.ShapeDtypeStruct((per, total, width), jnp.bfloat16),
            jax.ShapeDtypeStruct((per, panels, part, width), jnp.float32),
            jax.ShapeDtypeStruct((devices, per, pair_cap, width), jnp.float32),
        ],
        cost_estimate=pl.CostEstimate(
            flops=6 * per * total * (depth + panels * part) * width,
            transcendentals=0,
            bytes_accessed=16 * per * total * width,
        ),
        name="solve",
    )(flags, at, *args)


def lower_kernel(flag_ref, *refs, first, panels):
    x_ref, cross_ref, home_ref, swap_ref, a_high, a_low, b_high, b_low, c_high, c_low = refs[:10]
    rest = refs[10:] if first else refs[13:]
    high_ref, low_ref, alt_ref = rest[:3]
    group, _, part, width = x_ref.shape
    at_home = flag_ref[3] > 0
    even = flag_ref[4] > 0
    mine = jnp.where(at_home, x_ref[...].reshape(group * part, width), cross_ref[...])
    other = jnp.where(at_home, home_ref[...], swap_ref[...])
    left = dot3(*split(jnp.where(even, mine, other)), a_high[...], a_low[...])
    left_parts = split(left)
    right = jnp.where(even, other, mine) - dot3(*left_parts, c_high[...], c_low[...])
    right = dot3(*split(right), b_high[...], b_low[...])
    right_parts = split(right)
    panel = left.shape[1]
    high_ref[:, :panel], low_ref[:, :panel] = left_parts
    high_ref[:, panel:], low_ref[:, panel:] = right_parts
    alt_ref[...] = jnp.where(flag_ref[2] == 0, left, right)
    if first:
        old_high, old_low, old_alt = rest[3:]

        @pl.when(pl.program_id(0) == 0)
        def _():
            count = panels * part
            old_high[...] = high_ref[:count]
            old_low[...] = low_ref[:count]
            old_alt[...] = alt_ref[:count]


def lower(flags, x, band, bands, moved, factors, previous):
    blocks, _, part, width = x.shape
    panel = factors[0].shape[0]
    panels = 2
    size = blocks // bands
    group = max(g for g in range(1, size + 1) if size % g == 0 and (g * part <= 256 or g == 1))
    group = max(group, panels) if size % panels == 0 and band == 0 else group
    steps = size // group
    offset = band * steps
    whole = lambda j, *_: (0, 0)
    in_specs = [pl.BlockSpec((group, 1, part, width), lambda j, *_: (offset + j, 0, 0, 0))]
    in_specs += [pl.BlockSpec((group * part, width), lambda j, *_: (j, 0))] * 3
    in_specs += [pl.BlockSpec(factor.shape, whole) for factor in factors]
    args = [x, *moved, *factors]
    out_specs = [
        pl.BlockSpec((group * part, panels * panel), lambda j, *_: (offset + j, 0)),
        pl.BlockSpec((group * part, panels * panel), lambda j, *_: (offset + j, 0)),
        pl.BlockSpec((group * part, width), lambda j, *_: (offset + j, 0)),
    ]
    out_shape = [
        jax.ShapeDtypeStruct((blocks * part, panels * panel), jnp.bfloat16),
        jax.ShapeDtypeStruct((blocks * part, panels * panel), jnp.bfloat16),
        jax.ShapeDtypeStruct((blocks * part, width), jnp.float32),
    ]
    aliases = {}
    if previous is None:
        old = panels * part
        for shape, kind in (
            ((old, panels * panel), jnp.bfloat16),
            ((old, panels * panel), jnp.bfloat16),
            ((old, width), jnp.float32),
        ):
            out_specs.append(pl.BlockSpec(shape, whole))
            out_shape.append(jax.ShapeDtypeStruct(shape, kind))
    else:
        in_specs += [pl.BlockSpec(memory_space=pl.ANY)] * 3
        aliases = {1 + len(args) + index: index for index in range(3)}
        args += previous
    return pl.pallas_call(
        functools.partial(lower_kernel, first=previous is None, panels=panels),
        grid_spec=pltpu.PrefetchScalarGridSpec(
            num_scalar_prefetch=1, grid=(steps,), in_specs=in_specs, out_specs=out_specs
        ),
        out_shape=out_shape,
        input_output_aliases=aliases,
        cost_estimate=pl.CostEstimate(
            flops=18 * size * part * panel * panel, transcendentals=0, bytes_accessed=28 * size * part * width
        ),
        name="lower",
    )(flags, *args)


def trail_kernel(flag_ref, row_ref, slot_ref, count_ref, *refs, special):
    x_ref, l_high, l_low, u_high, u_low, front_ref, come_ref = refs[:7]
    rest = refs[7:]
    if special:
        alt_ref, corner_ref, rest = rest[0], rest[1], rest[2:]
    o_ref = rest[-1]
    group, _, part, width = x_ref.shape
    band = pl.program_id(0)
    value = x_ref[...].reshape(group * part, width) - dot3(l_high[...], l_low[...], u_high[0], u_low[0])
    if special:
        chosen = (flag_ref[1] > 0) & (pl.program_id(1) == 0)
        value = jnp.where(chosen, alt_ref[...], value)
    o_ref[:, 0] = value.reshape(group, part, width)

    @pl.when(band == 0)
    def _():
        for index in range(front_ref.shape[1]):
            front = front_ref[0, index]
            if special:
                front = jnp.where(chosen, corner_ref[index], front)
            o_ref[index, 0] = front

    devices, _, pair_cap, _ = come_ref.shape
    base = band * (devices * pair_cap)

    def body(index, _):
        spot = row_ref[base + index]
        slot = slot_ref[base + index]
        o_ref[spot // part, 0, pl.ds(spot % part, 1), :] = come_ref[slot // pair_cap, 0, pl.ds(slot % pair_cap, 1), :]
        return 0

    lax.fori_loop(0, count_ref[band], body, 0)


def trail(flags, tables, x, col, low, upper, front, come, special, previous, bands):
    blocks, _, part, width = x.shape
    per, total, _ = upper[0].shape
    group = blocks // bands
    in_specs = [
        pl.BlockSpec((group, 1, part, width), lambda j, i, *_: (j, col + i, 0, 0)),
        pl.BlockSpec((group * part, total), lambda j, i, *_: (j, 0)),
        pl.BlockSpec((group * part, total), lambda j, i, *_: (j, 0)),
        pl.BlockSpec((1, total, width), lambda j, i, *_: (i, 0, 0)),
        pl.BlockSpec((1, total, width), lambda j, i, *_: (i, 0, 0)),
        pl.BlockSpec((1,) + front.shape[1:], lambda j, i, *_: (i, 0, 0, 0)),
        pl.BlockSpec((come.shape[0], 1) + come.shape[2:], lambda j, i, *_: (0, i, 0, 0)),
    ]
    args = [x, *low, *upper, front, come]
    if special is not None:
        alt, corner = special
        in_specs.append(pl.BlockSpec((group * part, width), lambda j, i, *_: (j, 0)))
        in_specs.append(pl.BlockSpec(corner.shape, lambda j, i, *_: (0, 0, 0)))
        args += [alt, corner]
    aliases = {}
    if previous is not None:
        in_specs.append(pl.BlockSpec(memory_space=pl.ANY))
        args.append(previous)
        aliases = {4 + len(args) - 1: 0}
    return pl.pallas_call(
        functools.partial(trail_kernel, special=special is not None),
        grid_spec=pltpu.PrefetchScalarGridSpec(
            num_scalar_prefetch=4,
            grid=(bands, per),
            in_specs=in_specs,
            out_specs=pl.BlockSpec((group, 1, part, width), lambda j, i, *_: (j, col + i, 0, 0)),
        ),
        out_shape=jax.ShapeDtypeStruct(x.shape, jnp.float32),
        input_output_aliases=aliases,
        cost_estimate=pl.CostEstimate(
            flops=6 * per * blocks * part * total * width,
            transcendentals=0,
            bytes_accessed=16 * per * blocks * part * width,
        ),
        name="trail",
    )(flags, *tables, *args)


def ring_gather(own, devices):
    order = list(range(0, devices, 2)) + list(range(devices - 1, 0, -2))
    forward = [(order[i], order[(i + 1) % devices]) for i in range(devices)]
    backward = [(b, a) for a, b in forward]
    ahead = behind = own
    ahead_list, behind_list = [], []
    for _ in range(devices // 2 - 1):
        ahead = lax.ppermute(ahead, "prow", forward)
        behind = lax.ppermute(behind, "prow", backward)
        ahead_list.append(ahead)
        behind_list.append(behind)
    if own.shape[0] % 2 == 0:
        half = own.shape[0] // 2
        left, right = ahead[:half], behind[half:]
    else:
        half = own.shape[2] // 2
        left, right = ahead[:, :, :half], behind[:, :, half:]
    left = lax.ppermute(left, "prow", forward)
    right = lax.ppermute(right, "prow", backward)
    return [own, *ahead_list, *reversed(behind_list), left, right]


def row_moves(block, col_index, col_devices):
    moving = crossed = block
    for hop in range(1, col_devices // 2):
        moving = lax.ppermute(moving, "pcol", [(2 * hop - 2, 2 * hop), (2 * hop - 1, 2 * hop + 1)])
        crossed = moving if hop == 1 else jnp.where(col_index // 2 == hop, moving, crossed)
    home = lax.ppermute(block, "pcol", [(0, 1), (1, 0)])
    rest = [(i, i ^ 1) for i in range(2, col_devices)]
    if not rest:
        return crossed, home, home
    swap = lax.ppermute(crossed, "pcol", rest)
    return crossed, home, swap


def panel_pair(block, col_index, col_devices):
    crossed, home, swap = row_moves(block, col_index, col_devices)
    at_home = col_index < 2
    mine = jnp.where(at_home, block, crossed)
    other = jnp.where(at_home, home, swap)
    even = col_index % 2 == 0
    return jnp.where(even, mine, other), jnp.where(even, other, mine)


def chunking(cols):
    if cols < 4:
        return [1] * cols
    middle = cols // 2
    return [1, middle, cols - 1 - middle]


def fast(x, place, tables, lower_inv, upper_inv, sizes):
    panel, part, devices, cap, pair_cap, bands, rows = sizes
    send_at, out_at, in_tables = tables
    blocks, cols, _, width = x.shape
    panels = lower_inv.shape[0]
    row_index = lax.axis_index("prow")
    col_index = lax.axis_index("pcol")
    col_devices = lax.axis_size("pcol")
    widths = chunking(cols)
    chunks = [(sum(widths[:i]), per) for i, per in enumerate(widths)]
    flags = jnp.stack([row_index, col_index < panels, col_index, col_index < 2, col_index % 2 == 0]).astype(jnp.int32)
    raw = []
    for band in range(bands):
        block = x[band * (blocks // bands) : (band + 1) * (blocks // bands), 0].reshape(rows, width)
        raw.append(row_moves(block, col_index, col_devices))
    gathered = []
    for col, per in chunks:
        own = pack(send_at, x, col, per, cap)
        gathered.append(ring_gather(own, devices))
    head, sent = unpack(flags, place, gathered[0], cap, devices, panel)
    corner_low, corner_up = panel_pair(sent, col_index, col_devices)
    low_top = product(corner_low, upper_inv[0])
    up_side = product(lower_inv[0], corner_up)
    factors = [*halves(upper_inv[0]), *halves(upper_inv[1]), *halves(up_side)]
    low = old = None
    for band in range(bands):
        outs = lower(flags, x, band, bands, raw[band], factors, low)
        low = outs[:3]
        old = outs[3:] if band == 0 else old
    alt = low[2]
    select = (place[:, None] == jnp.arange(devices * cap, dtype=jnp.int32)[None, :]).astype(jnp.bfloat16)
    first = [
        jnp.dot(side, select[:panel], preferred_element_type=jnp.float32).astype(jnp.bfloat16)
        for side in halves(lower_inv[0])
    ]
    factors = [*first, select[panel:], *halves(low_top), *halves(lower_inv[1])]
    own_head = lax.dynamic_slice_in_dim(head, row_index * part, part, 0)
    own_tail = lax.dynamic_slice_in_dim(head, panel + row_index * part, part, 0)
    own_low = lax.dynamic_slice_in_dim(low_top, row_index * part, part, 0)
    own_up = lax.dynamic_slice_in_dim(up_side, row_index * part, part, 0)
    corner = jnp.where(
        col_index == 0, jnp.stack([own_head, own_low]), jnp.stack([own_up, own_tail - product(own_low, up_side)])
    )
    result = None
    for chunk, (col, per) in enumerate(chunks):
        u_high, u_low, front, send = solve(
            flags,
            out_at,
            factors,
            old[:2],
            x,
            col,
            gathered[chunk],
            old[2] if col == 0 else None,
            cap,
            devices,
            pair_cap,
            panels,
        )
        come = lax.all_to_all(send, "prow", 0, 0, tiled=True)
        special = (alt, corner) if col == 0 else None
        result = trail(flags, in_tables, x, col, low[:2], (u_high, u_low), front, come, special, result, bands)
    return result


def slow(x, wanted, came_from, pivots, lower_inv, upper_inv, result, sizes):
    panel, part, devices = sizes[:3]
    blocks, cols, _, width = x.shape
    total = wanted.shape[0]
    x = plain(x)
    row_index = lax.axis_index("prow")
    col_index = lax.axis_index("pcol")
    col_devices = lax.axis_size("pcol")
    rows = jnp.arange(blocks, dtype=jnp.int32)[:, None] * panel + jnp.arange(part, dtype=jnp.int32)[None, :]
    rows = (rows + row_index * part).reshape(-1)
    spots = jnp.where(came_from >= 0, pivots, blocks * panel)
    source = jnp.full((blocks * panel,), -1, jnp.int32).at[spots].set(came_from, mode="drop")[rows]
    needed = jnp.concatenate([wanted, jnp.arange(total, dtype=jnp.int32)])
    mine = (needed % panel // part == row_index)[:, None]
    spot = needed // panel * part + needed % part
    around = [(i, (i + 1) % devices) for i in range(devices)]

    def swapped(col):
        here = lax.dynamic_index_in_dim(x, col, 1, False).reshape(blocks * part, width)
        moving = jnp.where(mine, here[spot], 0.0)

        def hop(_, carry):
            moving, gathered = carry
            moving = lax.ppermute(moving, "prow", around)
            return moving, gathered + moving

        _, gathered = lax.fori_loop(0, devices - 1, hop, (moving, moving))
        head = gathered[:total]
        return head, jnp.where((source >= 0)[:, None], gathered[total:][jnp.maximum(source, 0)], here)

    head, body = swapped(0)
    raw = panel_pair(body, col_index, col_devices)
    corner = panel_pair(head, col_index, col_devices)
    low_top = product(corner[0][panel:], upper_inv[0])
    up_side = product(lower_inv[0], corner[1][:panel])
    low_first = product(raw[0], upper_inv[0])
    low_second = product(raw[1] - product(low_first, up_side), upper_inv[1])

    def column(col, result):
        head, body = swapped(col)
        upper = product(lower_inv[0], head[:panel])
        reduced = head[panel:] - product(low_top, upper)
        second = product(lower_inv[1], reduced)
        body = body - product(low_first, upper) - product(low_second, second)
        left = (col == 0) & (col_index == 0)
        right = (col == 0) & (col_index == 1)
        body = jnp.where(left, low_first, jnp.where(right, low_second, body))
        upper = jnp.where(left, head[:panel], upper)
        second = jnp.where(left, low_top, jnp.where(right, reduced, second))
        own = [lax.dynamic_slice_in_dim(side, row_index * part, part, 0) for side in (upper, second)]
        body = jnp.concatenate([*own, body[2 * part :]], axis=0)
        return plain(lax.dynamic_update_index_in_dim(plain(result), body.reshape(blocks, part, width), col, 1))

    return lax.fori_loop(0, cols, column, result)


def local(matrix, pivots, lower_inv, upper_inv):
    row_blocks, row_part, _, _ = matrix.shape
    panels, panel = pivots.shape
    devices = lax.axis_size("prow")
    total = panels * panel
    mean = total / devices
    cap = -(-int(mean + 2.75 * math.sqrt(mean)) // 8) * 8
    pair_mean = mean / devices
    pair_cap = -(-int(pair_mean + 4 * math.sqrt(pair_mean)) // 8) * 8
    bands = 2 if row_blocks % 2 == 0 else 1
    sizes = (panel, row_part, devices, cap, pair_cap, bands, row_blocks // bands * row_part)
    x = matrix.transpose(0, 2, 1, 3)
    me = lax.axis_index("prow").astype(jnp.int32).reshape(1)
    send_at, place, out_at, in_rows, in_slots, counts, over, wanted, came_from = routing(me, pivots, sizes)
    tables = (send_at[0], out_at[0], (in_rows[0], in_slots[0], counts[0]))
    result = fast(x, place[0], tables, lower_inv, upper_inv, sizes)

    def again(carry):
        _, result = carry
        result = slow(x, wanted[0], came_from[0], pivots.reshape(-1), lower_inv, upper_inv, result, sizes)
        return jnp.int32(-1), plain(result)

    _, result = lax.while_loop(lambda carry: carry[0] >= 0, again, (over[0, 0], plain(result)))
    return result.transpose(0, 2, 1, 3)


def solution(mesh):
    return jax.shard_map(
        local,
        mesh=mesh,
        in_specs=(P(None, "prow", None, "pcol"), P(), P(), P()),
        out_specs=P(None, "prow", None, "pcol"),
        check_vma=False,
    )
```

```python
import functools
import math

import jax
import jax.numpy as jnp
from jax import lax
from jax.experimental.layout import Layout, with_layout_constraint
from jax.experimental import pallas as pl
from jax.experimental.pallas import tpu as pltpu
from jax.sharding import PartitionSpec as P


def div_by(value, count):
    if count & (count - 1) == 0:
        return lax.shift_right_logical(value, jnp.full_like(value, count.bit_length() - 1))
    return lax.div(value, jnp.full_like(value, count))


def mod_by(value, count):
    if count & (count - 1) == 0:
        return value & (count - 1)
    return value - div_by(value, count) * count


def ring_place(index, count):
    return jnp.where(index % 2 == 0, index // 2, count - 1 - index // 2)


def split(value):
    high = value.astype(jnp.bfloat16)
    return high, (value - high.astype(jnp.float32)).astype(jnp.bfloat16)


def dot3(left_high, left_low, right_high, right_low):
    def one(left, right):
        return jnp.dot(left, right, preferred_element_type=jnp.float32)

    return one(left_high, right_high) + (one(left_high, right_low) + one(left_low, right_high))


def turned(row):
    return jnp.transpose(jnp.broadcast_to(row, (8, row.shape[1])))[:, :1]


def routing_kernel(
    me_ref,
    piv_row,
    piv_col,
    send_ref,
    place_ref,
    column_ref,
    out_ref,
    row_ref,
    slot_ref,
    count_ref,
    over_ref,
    want_ref,
    from_ref,
    *,
    sizes,
):
    panel, part, devices, cap, pair_cap, _, rows = sizes
    total = piv_row.shape[1]
    me = me_ref[0]
    p_row = piv_row[...]
    p_col = piv_col[...]
    lane = lax.broadcasted_iota(jnp.int32, (1, total), 1)
    sub = lax.broadcasted_iota(jnp.int32, (total, 1), 0)

    def top(mask, value):
        return jnp.max(jnp.where(mask, value, -1), axis=0, keepdims=True)

    def pick(index_row, value_col):
        return jnp.sum(jnp.where(sub == index_row, value_col, 0), axis=0, keepdims=True)

    chain = top((p_col == lane) & (sub < lane), sub)
    start = jnp.where(chain >= 0, chain, lane)

    def step(carry):
        pointer, _ = carry
        further = pick(pointer, turned(pointer))
        return further, jnp.max(jnp.abs(further - pointer))

    before, _ = lax.while_loop(lambda carry: carry[1] > 0, step, (start, jnp.int32(1)))
    same = p_col == p_row
    last = top(same & (sub < lane), sub)
    final = top(same, sub)
    wanted = jnp.where(last >= 0, pick(last, turned(before)), p_row)

    def owner(row):
        return div_by(mod_by(row, panel), part)

    def spot(row):
        return div_by(row, panel) * part + mod_by(row, part)

    holder = owner(wanted)
    rank = jnp.sum(jnp.where((turned(holder) == holder) & (sub < lane), 1, 0), axis=0, keepdims=True)
    moved = (final == lane) & (p_row >= total)
    source = owner(before)
    target = owner(p_row)
    pair = jnp.where(moved, source * devices + target, -1)
    pair_rank = jnp.sum(jnp.where((turned(pair) == pair) & (sub < lane), 1, 0), axis=0, keepdims=True)
    distance = ring_place(me, devices) - ring_place(holder, devices)
    distance = jnp.where(distance < 0, distance + devices, distance)
    place = distance * cap + rank
    place_ref[...] = place
    column_ref[...] = turned(place)

    def table(width, code, value):
        slots = lax.broadcasted_iota(jnp.int32, (1, width), 1)
        return jnp.sum(jnp.where(turned(code) == slots, turned(value), 0), axis=0, keepdims=True)

    send_ref[...] = table(send_ref.shape[1], jnp.where((holder == me) & (rank < cap), rank, -1), spot(wanted))
    want_ref[...] = wanted
    from_ref[...] = jnp.where(moved, before, -1)
    fits = moved & (pair_rank < pair_cap)
    going = fits & (source == me)
    coming = fits & (target == me)
    out_ref[...] = table(out_ref.shape[1], jnp.where(going, target * pair_cap + pair_rank, -1), spot(before))
    band = jnp.where(coming, div_by(spot(p_row), rows), -1)
    band_rank = jnp.sum(jnp.where((turned(band) == band) & (sub < lane), 1, 0), axis=0, keepdims=True)
    code = jnp.where(coming, band * (devices * pair_cap) + band_rank, -1)
    row_ref[...] = table(row_ref.shape[1], code, mod_by(spot(p_row), rows))
    slot_ref[...] = table(slot_ref.shape[1], code, source * pair_cap + pair_rank)
    kinds = lax.broadcasted_iota(jnp.int32, (1, count_ref.shape[1]), 1)
    count_ref[...] = jnp.sum(jnp.where(turned(band) == kinds, 1, 0), axis=0, keepdims=True)
    excess = jnp.maximum(jnp.max(rank) - cap, jnp.max(jnp.where(moved, pair_rank, 0)) - pair_cap)
    over_ref[...] = jnp.full(over_ref.shape, excess, jnp.int32)


def plain(value):
    return with_layout_constraint(value, Layout(major_to_minor=tuple(range(value.ndim))))


def lanes(count):
    return -(-count // 128) * 128


def routing(me, pivots, sizes):
    _, _, devices, cap, pair_cap, bands, _ = sizes
    total = pivots.size
    pairs = devices * pair_cap
    shapes = [lanes(cap), total, 0, lanes(pairs), lanes(bands * pairs), lanes(bands * pairs), 128, 128, total, total]
    return pl.pallas_call(
        functools.partial(routing_kernel, sizes=sizes),
        out_shape=[jax.ShapeDtypeStruct((1, width) if width else (total, 1), jnp.int32) for width in shapes],
        in_specs=[
            pl.BlockSpec(memory_space=pltpu.SMEM),
            pl.BlockSpec(memory_space=pltpu.VMEM),
            pl.BlockSpec(memory_space=pltpu.VMEM),
        ],
        name="routing",
    )(me, pivots.reshape(1, total), pivots.reshape(total, 1))


def move_rows(count, unroll, load, store):
    def body(step, _):
        rows = [step * unroll + inner for inner in range(unroll)]
        values = [load(row) for row in rows]
        for row, value in zip(rows, values):
            store(row, value)
        return 0

    lax.fori_loop(0, count // unroll, body, 0)


def pack_kernel(at_ref, x_ref, o_ref, *, part):
    def load(row):
        spot = at_ref[row]
        return x_ref[spot // part, 0, pl.ds(spot % part, 1), :]

    def store(row, value):
        o_ref[0, pl.ds(row, 1), :] = value

    move_rows(o_ref.shape[1], 8, load, store)


def pack(at, x, col, per, cap):
    blocks, _, part, width = x.shape
    return pl.pallas_call(
        functools.partial(pack_kernel, part=part),
        grid_spec=pltpu.PrefetchScalarGridSpec(
            num_scalar_prefetch=1,
            grid=(per,),
            in_specs=[pl.BlockSpec((blocks, 1, part, width), lambda i, at: (0, col + i, 0, 0))],
            out_specs=pl.BlockSpec((1, cap, width), lambda i, at: (i, 0, 0)),
        ),
        out_shape=jax.ShapeDtypeStruct((per, cap, width), jnp.float32),
        cost_estimate=pl.CostEstimate(flops=0, transcendentals=0, bytes_accessed=3 * per * blocks * part * width * 4),
        name="pack",
    )(at, x)


def piece_specs(pieces, offset):
    def spec(piece, start):
        count = piece.shape[0]
        return pl.BlockSpec((1,) + piece.shape[1:], lambda i, *_: (jnp.clip(i - start, 0, count - 1), 0, 0))

    per = pieces[0].shape[0]
    left, right = pieces[-2:]
    later = offset if left.shape[0] == per else offset + left.shape[0]
    return [spec(piece, offset) for piece in pieces[:-1]] + [spec(right, later)]


def load_pieces(pieces, cap, width, index, half, store):
    count = len(pieces) - 1
    far = (count + 1) // 2
    for place in range(count - 1):
        store((place if place < far else place + 1) * cap, 0, pieces[place][0])
    left, right = pieces[-2:]
    if left.shape[2] < width:
        store(far * cap, 0, left[0])
        store(far * cap, left.shape[2], right[0])
    else:
        store(far * cap, 0, jnp.where(index < half, left[0], right[0]))


def unpack_kernel(flag_ref, at_ref, *refs, cap):
    pieces, o_ref, sent_ref, buffer = refs[:-3], refs[-3], refs[-2], refs[-1]

    def put(row, col, value):
        buffer[row : row + value.shape[0], col : col + value.shape[1]] = value

    load_pieces(pieces, cap, buffer.shape[1], 0, 1, put)

    def load(row):
        return buffer[pl.ds(at_ref[row], 1), :]

    def store(row, value):
        o_ref[pl.ds(row, 1), :] = value

    move_rows(o_ref.shape[0], 8, load, store)
    panel = sent_ref.shape[0]
    sent_ref[...] = jnp.where(flag_ref[2] == 0, o_ref[panel:], o_ref[:panel])


def unpack(flags, at, pieces, cap, devices, panel):
    total = at.shape[0]
    _, _, width = pieces[0].shape
    return pl.pallas_call(
        functools.partial(unpack_kernel, cap=cap),
        grid_spec=pltpu.PrefetchScalarGridSpec(
            num_scalar_prefetch=2,
            grid=(1,),
            in_specs=piece_specs(pieces, 0),
            out_specs=[
                pl.BlockSpec((total, width), lambda i, *_: (0, 0)),
                pl.BlockSpec((panel, width), lambda i, *_: (0, 0)),
            ],
            scratch_shapes=[pltpu.VMEM((devices * cap, width), jnp.float32)],
        ),
        out_shape=[
            jax.ShapeDtypeStruct((total, width), jnp.float32),
            jax.ShapeDtypeStruct((panel, width), jnp.float32),
        ],
        cost_estimate=pl.CostEstimate(flops=0, transcendentals=0, bytes_accessed=16 * total * width),
        name="unpack",
    )(flags, at, *pieces)


def product_kernel(left_ref, right_ref, o_ref):
    o_ref[...] = dot3(*split(left_ref[...]), *split(right_ref[...]))


def product(left, right):
    rows, depth = left.shape
    width = right.shape[1]
    tile = math.gcd(rows, 32)
    return pl.pallas_call(
        product_kernel,
        grid=(rows // tile,),
        in_specs=[pl.BlockSpec((tile, depth), lambda i: (i, 0)), pl.BlockSpec((depth, width), lambda i: (0, 0))],
        out_specs=pl.BlockSpec((tile, width), lambda i: (i, 0)),
        out_shape=jax.ShapeDtypeStruct((rows, width), jnp.float32),
        name="product",
    )(left, right)


def select_kernel(place_ref, lower_ref, upper_ref, s_high, s_low, pick_ref, v_high, v_low, a_high, a_low, b_high, b_low):
    panel, depth = pick_ref.shape
    slots = lax.broadcasted_iota(jnp.int32, (1, depth), 1)
    chosen = jnp.where(place_ref[...] == slots, 1.0, 0.0).astype(jnp.bfloat16)
    pick_ref[...] = chosen[panel:]
    for target, side in zip((s_high, s_low), split(lower_ref[0])):
        target[...] = jnp.dot(side, chosen[:panel], preferred_element_type=jnp.float32).astype(jnp.bfloat16)
    v_high[...], v_low[...] = split(lower_ref[1])
    a_high[...], a_low[...] = split(upper_ref[0])
    b_high[...], b_low[...] = split(upper_ref[1])


def select(column, lower_inv, upper_inv, depth):
    panel = lower_inv.shape[1]
    shapes = [(panel, depth)] * 3 + [(panel, panel)] * 6
    return pl.pallas_call(
        select_kernel,
        in_specs=[pl.BlockSpec(memory_space=pltpu.VMEM)] * 3,
        out_shape=[jax.ShapeDtypeStruct(shape, jnp.bfloat16) for shape in shapes],
        name="select",
    )(column, lower_inv, upper_inv)


def corner_kernel(flag_ref, *refs):
    sent_ref, cross_ref, home_ref, swap_ref, lower_ref, a_high, a_low, top_ref, tail_ref = refs[:9]
    t_high, t_low, c_high, c_low, front_ref, low_full, up_full = refs[9:]
    at_home = flag_ref[3] > 0
    even = flag_ref[4] > 0
    mine = jnp.where(at_home, sent_ref[...], cross_ref[...])
    other = jnp.where(at_home, home_ref[...], swap_ref[...])
    low_full[...] = dot3(*split(jnp.where(even, mine, other)), a_high[...], a_low[...])
    up_full[...] = dot3(*split(lower_ref[0]), *split(jnp.where(even, other, mine)))
    t_high[...], t_low[...] = split(low_full[...])
    c_high[...], c_low[...] = split(up_full[...])
    part = top_ref.shape[0]
    start = pl.multiple_of(flag_ref[0] * part, 8)
    own_low = low_full[pl.ds(start, part), :]
    own_up = up_full[pl.ds(start, part), :]
    tail = tail_ref[...] - dot3(*split(own_low), c_high[...], c_low[...])
    first = flag_ref[2] == 0
    front_ref[0] = jnp.where(first, top_ref[...], own_up)
    front_ref[1] = jnp.where(first, own_low, tail)


def corner(flags, sent, moved, lower_inv, upper_parts, head, part):
    panel, width = sent.shape
    whole = lambda i, *_: (0, 0)
    square = pl.BlockSpec((panel, panel), whole)
    in_specs = [square] * 4 + [pl.BlockSpec((1, panel, panel), lambda i, *_: (0, 0, 0)), square, square]
    in_specs += [
        pl.BlockSpec((part, width), lambda i, flag: (flag[0], 0)),
        pl.BlockSpec((part, width), lambda i, flag: (panel // part + flag[0], 0)),
    ]
    return pl.pallas_call(
        corner_kernel,
        grid_spec=pltpu.PrefetchScalarGridSpec(
            num_scalar_prefetch=1,
            grid=(1,),
            in_specs=in_specs,
            out_specs=[square] * 4 + [pl.BlockSpec((2, part, width), lambda i, *_: (0, 0, 0))],
            scratch_shapes=[pltpu.VMEM((panel, panel), jnp.float32)] * 2,
        ),
        out_shape=[jax.ShapeDtypeStruct((panel, panel), jnp.bfloat16)] * 4
        + [jax.ShapeDtypeStruct((2, part, width), jnp.float32)],
        name="corner",
    )(flags, sent, *moved, lower_inv, *upper_parts, head, head)


def solve_kernel(flag_ref, at_ref, *refs, cap, widths, special):
    s_high, s_low, pick_ref, t_high, t_low, v_high, v_low, l_high, l_low, x_ref = refs[:10]
    pieces_count = (len(refs) - (19 if special else 18)) // len(widths)
    pieces = refs[10 : 10 + pieces_count * len(widths)]
    rest = refs[10 + pieces_count * len(widths) :]
    if special:
        alt_ref, rest = rest[0], rest[1:]
    u_high, u_low, front_ref, send_ref, g_high, g_low, u_full, y_ref = rest
    me = flag_ref[0]
    panel = pick_ref.shape[0]

    def put(row, col, value):
        high, low = split(value)
        g_high[row : row + value.shape[0], col : col + value.shape[1]] = high
        g_low[row : row + value.shape[0], col : col + value.shape[1]] = low

    offset = 0
    for chunk, per in enumerate(widths):
        index = pl.program_id(0) - offset

        @pl.when((index >= 0) & (index < per))
        def _():
            group = pieces[chunk * pieces_count : (chunk + 1) * pieces_count]
            load_pieces(group, cap, g_high.shape[1], index, per // 2, put)

        offset += per
    upper = dot3(s_high[...], s_low[...], g_high[...], g_low[...])
    u_full[:panel] = upper
    high, low = split(upper)
    u_high[0, :panel] = high
    u_low[0, :panel] = low
    picked = jnp.dot(pick_ref[...], g_high[...], preferred_element_type=jnp.float32)
    picked += jnp.dot(pick_ref[...], g_low[...], preferred_element_type=jnp.float32)
    reduced = picked - dot3(t_high[...], t_low[...], high, low)
    upper = dot3(v_high[...], v_low[...], *split(reduced))
    u_full[panel:] = upper
    high, low = split(upper)
    u_high[0, panel:] = high
    u_low[0, panel:] = low
    _, panels, part, width = front_ref.shape
    for index in range(panels):
        front_ref[0, index] = u_full[pl.ds(pl.multiple_of(index * panel + me * part, 8), part), :]
    old = x_ref[...].reshape(panels * part, width) - dot3(l_high[...], l_low[...], u_high[0], u_low[0])
    if special:
        old = jnp.where((flag_ref[1] > 0) & (pl.program_id(0) == 0), alt_ref[...], old)
    y_ref[...] = old
    devices, _, pair_cap, _ = send_ref.shape
    for target in range(devices):

        def load(row):
            return y_ref[pl.ds(at_ref[target * pair_cap + row], 1), :]

        def store(row, value):
            send_ref[target, 0, pl.ds(row, 1), :] = value

        move_rows(pair_cap, 8, load, store)


def solve(flags, at, factors, low, x, col, groups, alt, cap, devices, pair_cap, panels):
    panel, depth = factors[0].shape
    total = panels * panel
    _, _, part, width = x.shape
    widths = [pieces[0].shape[0] for pieces in groups]
    per = sum(widths)
    whole = lambda i, *_: (0, 0)
    in_specs = [pl.BlockSpec(factor.shape, whole) for factor in factors]
    in_specs += [
        pl.BlockSpec((panels * part, total), whole),
        pl.BlockSpec((panels * part, total), whole),
        pl.BlockSpec((panels, 1, part, width), lambda i, *_: (0, col + i, 0, 0)),
    ]
    args = [*factors, *low, x]
    for chunk, pieces in enumerate(groups):
        in_specs += piece_specs(pieces, sum(widths[:chunk]))
        args += pieces
    if alt is not None:
        in_specs.append(pl.BlockSpec((panels * part, width), whole))
        args.append(alt)
    return pl.pallas_call(
        functools.partial(solve_kernel, cap=cap, widths=widths, special=alt is not None),
        grid_spec=pltpu.PrefetchScalarGridSpec(
            num_scalar_prefetch=2,
            grid=(per,),
            in_specs=in_specs,
            out_specs=[
                pl.BlockSpec((1, total, width), lambda i, *_: (i, 0, 0)),
                pl.BlockSpec((1, total, width), lambda i, *_: (i, 0, 0)),
                pl.BlockSpec((1, panels, part, width), lambda i, *_: (i, 0, 0, 0)),
                pl.BlockSpec((devices, 1, pair_cap, width), lambda i, *_: (0, i, 0, 0)),
            ],
            scratch_shapes=[
                pltpu.VMEM((depth, width), jnp.bfloat16),
                pltpu.VMEM((depth, width), jnp.bfloat16),
                pltpu.VMEM((total, width), jnp.float32),
                pltpu.VMEM((panels * part, width), jnp.float32),
            ],
        ),
        out_shape=[
            jax.ShapeDtypeStruct((per, total, width), jnp.bfloat16),
            jax.ShapeDtypeStruct((per, total, width), jnp.bfloat16),
            jax.ShapeDtypeStruct((per, panels, part, width), jnp.float32),
            jax.ShapeDtypeStruct((devices, per, pair_cap, width), jnp.float32),
        ],
        cost_estimate=pl.CostEstimate(
            flops=6 * per * total * (depth + panels * part) * width,
            transcendentals=0,
            bytes_accessed=16 * per * total * width,
        ),
        name="solve",
    )(flags, at, *args)


def lower_kernel(flag_ref, *refs, first, panels):
    x_ref, cross_ref, home_ref, swap_ref, a_high, a_low, b_high, b_low, c_high, c_low = refs[:10]
    rest = refs[10:] if first else refs[13:]
    high_ref, low_ref, alt_ref = rest[:3]
    group, _, part, width = x_ref.shape
    at_home = flag_ref[3] > 0
    even = flag_ref[4] > 0
    mine = jnp.where(at_home, x_ref[...].reshape(group * part, width), cross_ref[...])
    other = jnp.where(at_home, home_ref[...], swap_ref[...])
    left = dot3(*split(jnp.where(even, mine, other)), a_high[...], a_low[...])
    left_parts = split(left)
    right = jnp.where(even, other, mine) - dot3(*left_parts, c_high[...], c_low[...])
    right = dot3(*split(right), b_high[...], b_low[...])
    right_parts = split(right)
    panel = left.shape[1]
    high_ref[:, :panel], low_ref[:, :panel] = left_parts
    high_ref[:, panel:], low_ref[:, panel:] = right_parts
    alt_ref[...] = jnp.where(flag_ref[2] == 0, left, right)
    if first:
        old_high, old_low, old_alt = rest[3:]

        @pl.when(pl.program_id(0) == 0)
        def _():
            count = panels * part
            old_high[...] = high_ref[:count]
            old_low[...] = low_ref[:count]
            old_alt[...] = alt_ref[:count]


def lower(flags, x, band, bands, moved, factors, previous):
    blocks, _, part, width = x.shape
    panel = factors[0].shape[0]
    panels = 2
    size = blocks // bands
    group = max(g for g in range(1, size + 1) if size % g == 0 and (g * part <= 256 or g == 1))
    group = max(group, panels) if size % panels == 0 and band == 0 else group
    steps = size // group
    offset = band * steps
    whole = lambda j, *_: (0, 0)
    in_specs = [pl.BlockSpec((group, 1, part, width), lambda j, *_: (offset + j, 0, 0, 0))]
    in_specs += [pl.BlockSpec((group * part, width), lambda j, *_: (j, 0))] * 3
    in_specs += [pl.BlockSpec(factor.shape, whole) for factor in factors]
    args = [x, *moved, *factors]
    out_specs = [
        pl.BlockSpec((group * part, panels * panel), lambda j, *_: (offset + j, 0)),
        pl.BlockSpec((group * part, panels * panel), lambda j, *_: (offset + j, 0)),
        pl.BlockSpec((group * part, width), lambda j, *_: (offset + j, 0)),
    ]
    out_shape = [
        jax.ShapeDtypeStruct((blocks * part, panels * panel), jnp.bfloat16),
        jax.ShapeDtypeStruct((blocks * part, panels * panel), jnp.bfloat16),
        jax.ShapeDtypeStruct((blocks * part, width), jnp.float32),
    ]
    aliases = {}
    if previous is None:
        old = panels * part
        for shape, kind in (
            ((old, panels * panel), jnp.bfloat16),
            ((old, panels * panel), jnp.bfloat16),
            ((old, width), jnp.float32),
        ):
            out_specs.append(pl.BlockSpec(shape, whole))
            out_shape.append(jax.ShapeDtypeStruct(shape, kind))
    else:
        in_specs += [pl.BlockSpec(memory_space=pl.ANY)] * 3
        aliases = {1 + len(args) + index: index for index in range(3)}
        args += previous
    return pl.pallas_call(
        functools.partial(lower_kernel, first=previous is None, panels=panels),
        grid_spec=pltpu.PrefetchScalarGridSpec(
            num_scalar_prefetch=1, grid=(steps,), in_specs=in_specs, out_specs=out_specs
        ),
        out_shape=out_shape,
        input_output_aliases=aliases,
        cost_estimate=pl.CostEstimate(
            flops=18 * size * part * panel * panel, transcendentals=0, bytes_accessed=28 * size * part * width
        ),
        name="lower",
    )(flags, *args)


def trail_kernel(flag_ref, row_ref, slot_ref, count_ref, *refs, special):
    x_ref, l_high, l_low, u_high, u_low, front_ref, come_ref = refs[:7]
    rest = refs[7:]
    if special:
        alt_ref, corner_ref, rest = rest[0], rest[1], rest[2:]
    o_ref = rest[-1]
    group, _, part, width = x_ref.shape
    band = pl.program_id(0)
    value = x_ref[...].reshape(group * part, width) - dot3(l_high[...], l_low[...], u_high[0], u_low[0])
    if special:
        chosen = (flag_ref[1] > 0) & (pl.program_id(1) == 0)
        value = jnp.where(chosen, alt_ref[...], value)
    o_ref[:, 0] = value.reshape(group, part, width)

    @pl.when(band == 0)
    def _():
        for index in range(front_ref.shape[1]):
            front = front_ref[0, index]
            if special:
                front = jnp.where(chosen, corner_ref[index], front)
            o_ref[index, 0] = front

    devices, _, pair_cap, _ = come_ref.shape
    base = band * (devices * pair_cap)

    def body(index, _):
        spot = row_ref[base + index]
        slot = slot_ref[base + index]
        o_ref[spot // part, 0, pl.ds(spot % part, 1), :] = come_ref[slot // pair_cap, 0, pl.ds(slot % pair_cap, 1), :]
        return 0

    lax.fori_loop(0, count_ref[band], body, 0)


def trail(flags, tables, x, col, low, upper, front, come, special, previous, bands):
    blocks, _, part, width = x.shape
    per, total, _ = upper[0].shape
    group = blocks // bands
    in_specs = [
        pl.BlockSpec((group, 1, part, width), lambda j, i, *_: (j, col + i, 0, 0)),
        pl.BlockSpec((group * part, total), lambda j, i, *_: (j, 0)),
        pl.BlockSpec((group * part, total), lambda j, i, *_: (j, 0)),
        pl.BlockSpec((1, total, width), lambda j, i, *_: (i, 0, 0)),
        pl.BlockSpec((1, total, width), lambda j, i, *_: (i, 0, 0)),
        pl.BlockSpec((1,) + front.shape[1:], lambda j, i, *_: (i, 0, 0, 0)),
        pl.BlockSpec((come.shape[0], 1) + come.shape[2:], lambda j, i, *_: (0, i, 0, 0)),
    ]
    args = [x, *low, *upper, front, come]
    if special is not None:
        alt, corner = special
        in_specs.append(pl.BlockSpec((group * part, width), lambda j, i, *_: (j, 0)))
        in_specs.append(pl.BlockSpec(corner.shape, lambda j, i, *_: (0, 0, 0)))
        args += [alt, corner]
    aliases = {}
    if previous is not None:
        in_specs.append(pl.BlockSpec(memory_space=pl.ANY))
        args.append(previous)
        aliases = {4 + len(args) - 1: 0}
    return pl.pallas_call(
        functools.partial(trail_kernel, special=special is not None),
        grid_spec=pltpu.PrefetchScalarGridSpec(
            num_scalar_prefetch=4,
            grid=(bands, per),
            in_specs=in_specs,
            out_specs=pl.BlockSpec((group, 1, part, width), lambda j, i, *_: (j, col + i, 0, 0)),
        ),
        out_shape=jax.ShapeDtypeStruct(x.shape, jnp.float32),
        input_output_aliases=aliases,
        cost_estimate=pl.CostEstimate(
            flops=6 * per * blocks * part * total * width,
            transcendentals=0,
            bytes_accessed=16 * per * blocks * part * width,
        ),
        name="trail",
    )(flags, *tables, *args)


def ring_gather(own, devices):
    order = list(range(0, devices, 2)) + list(range(devices - 1, 0, -2))
    forward = [(order[i], order[(i + 1) % devices]) for i in range(devices)]
    backward = [(b, a) for a, b in forward]
    ahead = behind = own
    ahead_list, behind_list = [], []
    for _ in range(devices // 2 - 1):
        ahead = lax.ppermute(ahead, "prow", forward)
        behind = lax.ppermute(behind, "prow", backward)
        ahead_list.append(ahead)
        behind_list.append(behind)
    if own.shape[0] % 2 == 0:
        half = own.shape[0] // 2
        left, right = ahead[:half], behind[half:]
    else:
        half = own.shape[2] // 2
        left, right = ahead[:, :, :half], behind[:, :, half:]
    left = lax.ppermute(left, "prow", forward)
    right = lax.ppermute(right, "prow", backward)
    return [own, *ahead_list, *reversed(behind_list), left, right]


def row_moves(block, col_index, col_devices):
    moving = crossed = block
    for hop in range(1, col_devices // 2):
        moving = lax.ppermute(moving, "pcol", [(2 * hop - 2, 2 * hop), (2 * hop - 1, 2 * hop + 1)])
        crossed = moving if hop == 1 else jnp.where(col_index // 2 == hop, moving, crossed)
    home = lax.ppermute(block, "pcol", [(0, 1), (1, 0)])
    rest = [(i, i ^ 1) for i in range(2, col_devices)]
    if not rest:
        return crossed, home, home
    swap = lax.ppermute(crossed, "pcol", rest)
    return crossed, home, swap


def panel_pair(block, col_index, col_devices):
    crossed, home, swap = row_moves(block, col_index, col_devices)
    at_home = col_index < 2
    mine = jnp.where(at_home, block, crossed)
    other = jnp.where(at_home, home, swap)
    even = col_index % 2 == 0
    return jnp.where(even, mine, other), jnp.where(even, other, mine)


def chunking(cols):
    if cols < 4:
        return [1] * cols
    middle = cols // 2
    return [1, middle, cols - 1 - middle]


def grouping(chunks):
    return [[chunk] for chunk in range(chunks)]


def fast(x, place, column, tables, lower_inv, upper_inv, sizes):
    panel, part, devices, cap, pair_cap, bands, rows = sizes
    send_at, out_at, in_tables = tables
    blocks, cols, _, width = x.shape
    panels = lower_inv.shape[0]
    row_index = lax.axis_index("prow")
    col_index = lax.axis_index("pcol")
    col_devices = lax.axis_size("pcol")
    widths = chunking(cols)
    chunks = [(sum(widths[:i]), per) for i, per in enumerate(widths)]
    flags = jnp.stack([row_index, col_index < panels, col_index, col_index < 2, col_index % 2 == 0]).astype(jnp.int32)
    raw = []
    for band in range(bands):
        block = x[band * (blocks // bands) : (band + 1) * (blocks // bands), 0].reshape(rows, width)
        raw.append(row_moves(block, col_index, col_devices))
    gathered = []
    for col, per in chunks:
        own = pack(send_at, x, col, per, cap)
        gathered.append(ring_gather(own, devices))
    head, sent = unpack(flags, place, gathered[0], cap, devices, panel)
    parts = select(column, lower_inv, upper_inv, devices * cap)
    s_high, s_low, pick, v_high, v_low = parts[:5]
    upper_parts = parts[5:]
    moved = row_moves(sent, col_index, col_devices)
    t_high, t_low, c_high, c_low, front_corner = corner(flags, sent, moved, lower_inv, upper_parts[:2], head, part)
    low = old = None
    for band in range(bands):
        outs = lower(flags, x, band, bands, raw[band], [*upper_parts, c_high, c_low], low)
        low = outs[:3]
        old = outs[3:] if band == 0 else old
    alt = low[2]
    factors = [s_high, s_low, pick, t_high, t_low, v_high, v_low]
    result = None
    for group in grouping(len(chunks)):
        col = chunks[group[0]][0]
        u_high, u_low, front, send = solve(
            flags,
            out_at,
            factors,
            old[:2],
            x,
            col,
            [gathered[chunk] for chunk in group],
            old[2] if col == 0 else None,
            cap,
            devices,
            pair_cap,
            panels,
        )
        come = lax.all_to_all(send, "prow", 0, 0, tiled=True)
        special = (alt, front_corner) if col == 0 else None
        result = trail(flags, in_tables, x, col, low[:2], (u_high, u_low), front, come, special, result, bands)
    return result


def slow(x, wanted, came_from, pivots, lower_inv, upper_inv, result, sizes):
    panel, part, devices = sizes[:3]
    blocks, cols, _, width = x.shape
    total = wanted.shape[0]
    x = plain(x)
    row_index = lax.axis_index("prow")
    col_index = lax.axis_index("pcol")
    col_devices = lax.axis_size("pcol")
    rows = jnp.arange(blocks, dtype=jnp.int32)[:, None] * panel + jnp.arange(part, dtype=jnp.int32)[None, :]
    rows = (rows + row_index * part).reshape(-1)
    spots = jnp.where(came_from >= 0, pivots, blocks * panel)
    source = jnp.full((blocks * panel,), -1, jnp.int32).at[spots].set(came_from, mode="drop")[rows]
    needed = jnp.concatenate([wanted, jnp.arange(total, dtype=jnp.int32)])
    mine = (needed % panel // part == row_index)[:, None]
    spot = needed // panel * part + needed % part
    around = [(i, (i + 1) % devices) for i in range(devices)]

    def swapped(col):
        here = lax.dynamic_index_in_dim(x, col, 1, False).reshape(blocks * part, width)
        moving = jnp.where(mine, here[spot], 0.0)

        def hop(_, carry):
            moving, gathered = carry
            moving = lax.ppermute(moving, "prow", around)
            return moving, gathered + moving

        _, gathered = lax.fori_loop(0, devices - 1, hop, (moving, moving))
        head = gathered[:total]
        return head, jnp.where((source >= 0)[:, None], gathered[total:][jnp.maximum(source, 0)], here)

    head, body = swapped(0)
    raw = panel_pair(body, col_index, col_devices)
    corner = panel_pair(head, col_index, col_devices)
    low_top = product(corner[0][panel:], upper_inv[0])
    up_side = product(lower_inv[0], corner[1][:panel])
    low_first = product(raw[0], upper_inv[0])
    low_second = product(raw[1] - product(low_first, up_side), upper_inv[1])

    def column(col, result):
        head, body = swapped(col)
        upper = product(lower_inv[0], head[:panel])
        reduced = head[panel:] - product(low_top, upper)
        second = product(lower_inv[1], reduced)
        body = body - product(low_first, upper) - product(low_second, second)
        left = (col == 0) & (col_index == 0)
        right = (col == 0) & (col_index == 1)
        body = jnp.where(left, low_first, jnp.where(right, low_second, body))
        upper = jnp.where(left, head[:panel], upper)
        second = jnp.where(left, low_top, jnp.where(right, reduced, second))
        own = [lax.dynamic_slice_in_dim(side, row_index * part, part, 0) for side in (upper, second)]
        body = jnp.concatenate([*own, body[2 * part :]], axis=0)
        return plain(lax.dynamic_update_index_in_dim(plain(result), body.reshape(blocks, part, width), col, 1))

    return lax.fori_loop(0, cols, column, result)


def local(matrix, pivots, lower_inv, upper_inv):
    row_blocks, row_part, _, _ = matrix.shape
    panels, panel = pivots.shape
    devices = lax.axis_size("prow")
    total = panels * panel
    mean = total / devices
    cap = -(-int(mean + 2.75 * math.sqrt(mean)) // 8) * 8
    pair_mean = mean / devices
    pair_cap = -(-int(pair_mean + 4 * math.sqrt(pair_mean)) // 8) * 8
    bands = 2 if row_blocks % 2 == 0 else 1
    sizes = (panel, row_part, devices, cap, pair_cap, bands, row_blocks // bands * row_part)
    x = matrix.transpose(0, 2, 1, 3)
    me = lax.axis_index("prow").astype(jnp.int32).reshape(1)
    send_at, place, column, out_at, in_rows, in_slots, counts, over, wanted, came_from = routing(me, pivots, sizes)
    tables = (send_at[0], out_at[0], (in_rows[0], in_slots[0], counts[0]))
    result = fast(x, place[0], column, tables, lower_inv, upper_inv, sizes)

    def again(carry):
        _, result = carry
        result = slow(x, wanted[0], came_from[0], pivots.reshape(-1), lower_inv, upper_inv, result, sizes)
        return jnp.int32(-1), plain(result)

    _, result = lax.while_loop(lambda carry: carry[0] >= 0, again, (over[0, 0], plain(result)))
    return result.transpose(0, 2, 1, 3)


def solution(mesh):
    return jax.shard_map(
        local,
        mesh=mesh,
        in_specs=(P(None, "prow", None, "pcol"), P(), P(), P()),
        out_specs=P(None, "prow", None, "pcol"),
        check_vma=False,
    )
```

```python
import functools
import math

import jax
import jax.numpy as jnp
from jax import lax
from jax.experimental.layout import Layout, with_layout_constraint
from jax.experimental import pallas as pl
from jax.experimental.pallas import tpu as pltpu
from jax.sharding import PartitionSpec as P


def div_by(value, count):
    if count & (count - 1) == 0:
        return lax.shift_right_logical(value, jnp.full_like(value, count.bit_length() - 1))
    return lax.div(value, jnp.full_like(value, count))


def mod_by(value, count):
    if count & (count - 1) == 0:
        return value & (count - 1)
    return value - div_by(value, count) * count


def ring_place(index, count):
    return jnp.where(index % 2 == 0, index // 2, count - 1 - index // 2)


def split(value):
    high = value.astype(jnp.bfloat16)
    return high, (value - high.astype(jnp.float32)).astype(jnp.bfloat16)


def dot3(left_high, left_low, right_high, right_low):
    def one(left, right):
        return jnp.dot(left, right, preferred_element_type=jnp.float32)

    return one(left_high, right_high) + (one(left_high, right_low) + one(left_low, right_high))


def turned(row):
    return jnp.transpose(jnp.broadcast_to(row, (8, row.shape[1])))[:, :1]


def routing_kernel(
    me_ref,
    piv_ref,
    send_ref,
    place_ref,
    column_ref,
    out_ref,
    row_ref,
    slot_ref,
    count_ref,
    over_ref,
    want_ref,
    from_ref,
    *,
    sizes,
):
    panel, part, devices, cap, pair_cap, _, rows = sizes
    total = piv_ref.shape[0] * piv_ref.shape[1]
    me = me_ref[0]
    p_row = jnp.concatenate([piv_ref[index : index + 1, :] for index in range(piv_ref.shape[0])], axis=1)
    p_col = turned(p_row)
    lane = lax.broadcasted_iota(jnp.int32, (1, total), 1)
    sub = lax.broadcasted_iota(jnp.int32, (total, 1), 0)

    def top(mask, value):
        return jnp.max(jnp.where(mask, value, -1), axis=0, keepdims=True)

    def pick(index_row, value_col):
        return jnp.sum(jnp.where(sub == index_row, value_col, 0), axis=0, keepdims=True)

    chain = top((p_col == lane) & (sub < lane), sub)
    start = jnp.where(chain >= 0, chain, lane)

    def step(carry):
        pointer, _ = carry
        further = pick(pointer, turned(pointer))
        return further, jnp.max(jnp.abs(further - pointer))

    before, _ = lax.while_loop(lambda carry: carry[1] > 0, step, (start, jnp.int32(1)))
    same = p_col == p_row
    last = top(same & (sub < lane), sub)
    final = top(same, sub)
    wanted = jnp.where(last >= 0, pick(last, turned(before)), p_row)

    def owner(row):
        return div_by(mod_by(row, panel), part)

    def spot(row):
        return div_by(row, panel) * part + mod_by(row, part)

    holder = owner(wanted)
    rank = jnp.sum(jnp.where((turned(holder) == holder) & (sub < lane), 1, 0), axis=0, keepdims=True)
    moved = (final == lane) & (p_row >= total)
    source = owner(before)
    target = owner(p_row)
    pair = jnp.where(moved, source * devices + target, -1)
    pair_rank = jnp.sum(jnp.where((turned(pair) == pair) & (sub < lane), 1, 0), axis=0, keepdims=True)
    distance = ring_place(me, devices) - ring_place(holder, devices)
    distance = jnp.where(distance < 0, distance + devices, distance)
    place = distance * cap + rank
    place_ref[...] = place
    column_ref[...] = turned(place)

    def table(width, code, value):
        slots = lax.broadcasted_iota(jnp.int32, (1, width), 1)
        return jnp.sum(jnp.where(turned(code) == slots, turned(value), 0), axis=0, keepdims=True)

    send_ref[...] = table(send_ref.shape[1], jnp.where((holder == me) & (rank < cap), rank, -1), spot(wanted))
    want_ref[...] = wanted
    from_ref[...] = jnp.where(moved, before, -1)
    fits = moved & (pair_rank < pair_cap)
    going = fits & (source == me)
    coming = fits & (target == me)
    out_ref[...] = table(out_ref.shape[1], jnp.where(going, target * pair_cap + pair_rank, -1), spot(before))
    band = jnp.where(coming, div_by(spot(p_row), rows), -1)
    band_rank = jnp.sum(jnp.where((turned(band) == band) & (sub < lane), 1, 0), axis=0, keepdims=True)
    code = jnp.where(coming, band * (devices * pair_cap) + band_rank, -1)
    row_ref[...] = table(row_ref.shape[1], code, mod_by(spot(p_row), rows))
    slot_ref[...] = table(slot_ref.shape[1], code, source * pair_cap + pair_rank)
    kinds = lax.broadcasted_iota(jnp.int32, (1, count_ref.shape[1]), 1)
    count_ref[...] = jnp.sum(jnp.where(turned(band) == kinds, 1, 0), axis=0, keepdims=True)
    excess = jnp.maximum(jnp.max(rank) - cap, jnp.max(jnp.where(moved, pair_rank, 0)) - pair_cap)
    over_ref[...] = jnp.full(over_ref.shape, excess, jnp.int32)


def plain(value):
    return with_layout_constraint(value, Layout(major_to_minor=tuple(range(value.ndim))))


def lanes(count):
    return -(-count // 128) * 128


def routing(me, pivots, sizes):
    _, _, devices, cap, pair_cap, bands, _ = sizes
    total = pivots.size
    pairs = devices * pair_cap
    shapes = [lanes(cap), total, 0, lanes(pairs), lanes(bands * pairs), lanes(bands * pairs), 128, 128, total, total]
    return pl.pallas_call(
        functools.partial(routing_kernel, sizes=sizes),
        out_shape=[jax.ShapeDtypeStruct((1, width) if width else (total, 1), jnp.int32) for width in shapes],
        in_specs=[
            pl.BlockSpec(memory_space=pltpu.SMEM),
            pl.BlockSpec(memory_space=pltpu.VMEM),
        ],
        name="routing",
    )(me, pivots)


def move_rows(count, unroll, load, store):
    def body(step, _):
        rows = [step * unroll + inner for inner in range(unroll)]
        values = [load(row) for row in rows]
        for row, value in zip(rows, values):
            store(row, value)
        return 0

    lax.fori_loop(0, count // unroll, body, 0)


def pack_kernel(at_ref, x_ref, o_ref, *, part):
    def load(row):
        spot = at_ref[row]
        return x_ref[spot // part, 0, pl.ds(spot % part, 1), :]

    def store(row, value):
        o_ref[0, pl.ds(row, 1), :] = value

    move_rows(o_ref.shape[1], 8, load, store)


def pack(at, x, col, per, cap):
    blocks, _, part, width = x.shape
    return pl.pallas_call(
        functools.partial(pack_kernel, part=part),
        grid_spec=pltpu.PrefetchScalarGridSpec(
            num_scalar_prefetch=1,
            grid=(per,),
            in_specs=[pl.BlockSpec((blocks, 1, part, width), lambda i, at: (0, col + i, 0, 0))],
            out_specs=pl.BlockSpec((1, cap, width), lambda i, at: (i, 0, 0)),
        ),
        out_shape=jax.ShapeDtypeStruct((per, cap, width), jnp.float32),
        cost_estimate=pl.CostEstimate(flops=0, transcendentals=0, bytes_accessed=3 * per * blocks * part * width * 4),
        name="pack",
    )(at, x)


def piece_specs(pieces, offset):
    def spec(piece, start):
        count = piece.shape[0]
        return pl.BlockSpec((1,) + piece.shape[1:], lambda i, *_: (jnp.clip(i - start, 0, count - 1), 0, 0))

    per = pieces[0].shape[0]
    left, right = pieces[-2:]
    later = offset if left.shape[0] == per else offset + left.shape[0]
    return [spec(piece, offset) for piece in pieces[:-1]] + [spec(right, later)]


def load_pieces(pieces, cap, width, index, half, store):
    count = len(pieces) - 1
    far = (count + 1) // 2
    for place in range(count - 1):
        store((place if place < far else place + 1) * cap, 0, pieces[place][0])
    left, right = pieces[-2:]
    if left.shape[2] < width:
        store(far * cap, 0, left[0])
        store(far * cap, left.shape[2], right[0])
    else:
        store(far * cap, 0, jnp.where(index < half, left[0], right[0]))


def unpack_kernel(flag_ref, at_ref, *refs, cap):
    pieces, o_ref, sent_ref, buffer = refs[:-3], refs[-3], refs[-2], refs[-1]

    def put(row, col, value):
        buffer[row : row + value.shape[0], col : col + value.shape[1]] = value

    load_pieces(pieces, cap, buffer.shape[1], 0, 1, put)

    def load(row):
        return buffer[pl.ds(at_ref[row], 1), :]

    def store(row, value):
        o_ref[pl.ds(row, 1), :] = value

    move_rows(o_ref.shape[0], 8, load, store)
    panel = sent_ref.shape[0]
    sent_ref[...] = jnp.where(flag_ref[2] == 0, o_ref[panel:], o_ref[:panel])


def unpack(flags, at, pieces, cap, devices, panel):
    total = at.shape[0]
    _, _, width = pieces[0].shape
    return pl.pallas_call(
        functools.partial(unpack_kernel, cap=cap),
        grid_spec=pltpu.PrefetchScalarGridSpec(
            num_scalar_prefetch=2,
            grid=(1,),
            in_specs=piece_specs(pieces, 0),
            out_specs=[
                pl.BlockSpec((total, width), lambda i, *_: (0, 0)),
                pl.BlockSpec((panel, width), lambda i, *_: (0, 0)),
            ],
            scratch_shapes=[pltpu.VMEM((devices * cap, width), jnp.float32)],
        ),
        out_shape=[
            jax.ShapeDtypeStruct((total, width), jnp.float32),
            jax.ShapeDtypeStruct((panel, width), jnp.float32),
        ],
        cost_estimate=pl.CostEstimate(flops=0, transcendentals=0, bytes_accessed=16 * total * width),
        name="unpack",
    )(flags, at, *pieces)


def product_kernel(left_ref, right_ref, o_ref):
    o_ref[...] = dot3(*split(left_ref[...]), *split(right_ref[...]))


def product(left, right):
    rows, depth = left.shape
    width = right.shape[1]
    tile = math.gcd(rows, 32)
    return pl.pallas_call(
        product_kernel,
        grid=(rows // tile,),
        in_specs=[pl.BlockSpec((tile, depth), lambda i: (i, 0)), pl.BlockSpec((depth, width), lambda i: (0, 0))],
        out_specs=pl.BlockSpec((tile, width), lambda i: (i, 0)),
        out_shape=jax.ShapeDtypeStruct((rows, width), jnp.float32),
        name="product",
    )(left, right)


def select_kernel(place_ref, lower_ref, upper_ref, s_high, s_low, pick_ref, v_high, v_low, a_high, a_low, b_high, b_low):
    panel, depth = pick_ref.shape
    slots = lax.broadcasted_iota(jnp.int32, (1, depth), 1)
    chosen = jnp.where(place_ref[...] == slots, 1.0, 0.0).astype(jnp.bfloat16)
    pick_ref[...] = chosen[panel:]
    for target, side in zip((s_high, s_low), split(lower_ref[0])):
        target[...] = jnp.dot(side, chosen[:panel], preferred_element_type=jnp.float32).astype(jnp.bfloat16)
    v_high[...], v_low[...] = split(lower_ref[1])
    a_high[...], a_low[...] = split(upper_ref[0])
    b_high[...], b_low[...] = split(upper_ref[1])


def select(column, lower_inv, upper_inv, depth):
    panel = lower_inv.shape[1]
    shapes = [(panel, depth)] * 3 + [(panel, panel)] * 6
    return pl.pallas_call(
        select_kernel,
        in_specs=[pl.BlockSpec(memory_space=pltpu.VMEM)] * 3,
        out_shape=[jax.ShapeDtypeStruct(shape, jnp.bfloat16) for shape in shapes],
        name="select",
    )(column, lower_inv, upper_inv)


def corner_kernel(flag_ref, *refs):
    sent_ref, cross_ref, home_ref, swap_ref, lower_ref, a_high, a_low, top_ref, tail_ref = refs[:9]
    t_high, t_low, c_high, c_low, front_ref, low_full, up_full = refs[9:]
    at_home = flag_ref[3] > 0
    even = flag_ref[4] > 0
    mine = jnp.where(at_home, sent_ref[...], cross_ref[...])
    other = jnp.where(at_home, home_ref[...], swap_ref[...])
    low_full[...] = dot3(*split(jnp.where(even, mine, other)), a_high[...], a_low[...])
    up_full[...] = dot3(*split(lower_ref[0]), *split(jnp.where(even, other, mine)))
    t_high[...], t_low[...] = split(low_full[...])
    c_high[...], c_low[...] = split(up_full[...])
    part = top_ref.shape[0]
    start = pl.multiple_of(flag_ref[0] * part, 8)
    own_low = low_full[pl.ds(start, part), :]
    own_up = up_full[pl.ds(start, part), :]
    tail = tail_ref[...] - dot3(*split(own_low), c_high[...], c_low[...])
    first = flag_ref[2] == 0
    front_ref[0] = jnp.where(first, top_ref[...], own_up)
    front_ref[1] = jnp.where(first, own_low, tail)


def corner(flags, sent, moved, lower_inv, upper_parts, head, part):
    panel, width = sent.shape
    whole = lambda i, *_: (0, 0)
    square = pl.BlockSpec((panel, panel), whole)
    in_specs = [square] * 4 + [pl.BlockSpec((1, panel, panel), lambda i, *_: (0, 0, 0)), square, square]
    in_specs += [
        pl.BlockSpec((part, width), lambda i, flag: (flag[0], 0)),
        pl.BlockSpec((part, width), lambda i, flag: (panel // part + flag[0], 0)),
    ]
    return pl.pallas_call(
        corner_kernel,
        grid_spec=pltpu.PrefetchScalarGridSpec(
            num_scalar_prefetch=1,
            grid=(1,),
            in_specs=in_specs,
            out_specs=[square] * 4 + [pl.BlockSpec((2, part, width), lambda i, *_: (0, 0, 0))],
            scratch_shapes=[pltpu.VMEM((panel, panel), jnp.float32)] * 2,
        ),
        out_shape=[jax.ShapeDtypeStruct((panel, panel), jnp.bfloat16)] * 4
        + [jax.ShapeDtypeStruct((2, part, width), jnp.float32)],
        name="corner",
    )(flags, sent, *moved, lower_inv, *upper_parts, head, head)


def solve_kernel(flag_ref, at_ref, *refs, cap, widths, special):
    s_high, s_low, pick_ref, t_high, t_low, v_high, v_low, l_high, l_low, x_ref = refs[:10]
    pieces_count = (len(refs) - (19 if special else 18)) // len(widths)
    pieces = refs[10 : 10 + pieces_count * len(widths)]
    rest = refs[10 + pieces_count * len(widths) :]
    if special:
        alt_ref, rest = rest[0], rest[1:]
    u_high, u_low, front_ref, send_ref, g_high, g_low, u_full, y_ref = rest
    me = flag_ref[0]
    panel = pick_ref.shape[0]

    def put(row, col, value):
        high, low = split(value)
        g_high[row : row + value.shape[0], col : col + value.shape[1]] = high
        g_low[row : row + value.shape[0], col : col + value.shape[1]] = low

    offset = 0
    for chunk, per in enumerate(widths):
        index = pl.program_id(0) - offset

        @pl.when((index >= 0) & (index < per))
        def _():
            group = pieces[chunk * pieces_count : (chunk + 1) * pieces_count]
            load_pieces(group, cap, g_high.shape[1], index, per // 2, put)

        offset += per
    upper = dot3(s_high[...], s_low[...], g_high[...], g_low[...])
    u_full[:panel] = upper
    high, low = split(upper)
    u_high[0, :panel] = high
    u_low[0, :panel] = low
    picked = jnp.dot(pick_ref[...], g_high[...], preferred_element_type=jnp.float32)
    picked += jnp.dot(pick_ref[...], g_low[...], preferred_element_type=jnp.float32)
    reduced = picked - dot3(t_high[...], t_low[...], high, low)
    upper = dot3(v_high[...], v_low[...], *split(reduced))
    u_full[panel:] = upper
    high, low = split(upper)
    u_high[0, panel:] = high
    u_low[0, panel:] = low
    _, panels, part, width = front_ref.shape
    for index in range(panels):
        front_ref[0, index] = u_full[pl.ds(pl.multiple_of(index * panel + me * part, 8), part), :]
    old = x_ref[...].reshape(panels * part, width) - dot3(l_high[...], l_low[...], u_high[0], u_low[0])
    if special:
        old = jnp.where((flag_ref[1] > 0) & (pl.program_id(0) == 0), alt_ref[...], old)
    y_ref[...] = old
    devices, _, pair_cap, _ = send_ref.shape
    for target in range(devices):

        def load(row):
            return y_ref[pl.ds(at_ref[target * pair_cap + row], 1), :]

        def store(row, value):
            send_ref[target, 0, pl.ds(row, 1), :] = value

        move_rows(pair_cap, 8, load, store)


def solve(flags, at, factors, low, x, col, groups, alt, cap, devices, pair_cap, panels):
    panel, depth = factors[0].shape
    total = panels * panel
    _, _, part, width = x.shape
    widths = [pieces[0].shape[0] for pieces in groups]
    per = sum(widths)
    whole = lambda i, *_: (0, 0)
    in_specs = [pl.BlockSpec(factor.shape, whole) for factor in factors]
    in_specs += [
        pl.BlockSpec((panels * part, total), whole),
        pl.BlockSpec((panels * part, total), whole),
        pl.BlockSpec((panels, 1, part, width), lambda i, *_: (0, col + i, 0, 0)),
    ]
    args = [*factors, *low, x]
    for chunk, pieces in enumerate(groups):
        in_specs += piece_specs(pieces, sum(widths[:chunk]))
        args += pieces
    if alt is not None:
        in_specs.append(pl.BlockSpec((panels * part, width), whole))
        args.append(alt)
    return pl.pallas_call(
        functools.partial(solve_kernel, cap=cap, widths=widths, special=alt is not None),
        grid_spec=pltpu.PrefetchScalarGridSpec(
            num_scalar_prefetch=2,
            grid=(per,),
            in_specs=in_specs,
            out_specs=[
                pl.BlockSpec((1, total, width), lambda i, *_: (i, 0, 0)),
                pl.BlockSpec((1, total, width), lambda i, *_: (i, 0, 0)),
                pl.BlockSpec((1, panels, part, width), lambda i, *_: (i, 0, 0, 0)),
                pl.BlockSpec((devices, 1, pair_cap, width), lambda i, *_: (0, i, 0, 0)),
            ],
            scratch_shapes=[
                pltpu.VMEM((depth, width), jnp.bfloat16),
                pltpu.VMEM((depth, width), jnp.bfloat16),
                pltpu.VMEM((total, width), jnp.float32),
                pltpu.VMEM((panels * part, width), jnp.float32),
            ],
        ),
        out_shape=[
            jax.ShapeDtypeStruct((per, total, width), jnp.bfloat16),
            jax.ShapeDtypeStruct((per, total, width), jnp.bfloat16),
            jax.ShapeDtypeStruct((per, panels, part, width), jnp.float32),
            jax.ShapeDtypeStruct((devices, per, pair_cap, width), jnp.float32),
        ],
        cost_estimate=pl.CostEstimate(
            flops=6 * per * total * (depth + panels * part) * width,
            transcendentals=0,
            bytes_accessed=16 * per * total * width,
        ),
        name="solve",
    )(flags, at, *args)


def lower_kernel(flag_ref, *refs, first, panels):
    x_ref, cross_ref, home_ref, swap_ref, a_high, a_low, b_high, b_low, c_high, c_low = refs[:10]
    rest = refs[10:] if first else refs[13:]
    high_ref, low_ref, alt_ref = rest[:3]
    group, _, part, width = x_ref.shape
    at_home = flag_ref[3] > 0
    even = flag_ref[4] > 0
    mine = jnp.where(at_home, x_ref[...].reshape(group * part, width), cross_ref[...])
    other = jnp.where(at_home, home_ref[...], swap_ref[...])
    left = dot3(*split(jnp.where(even, mine, other)), a_high[...], a_low[...])
    left_parts = split(left)
    right = jnp.where(even, other, mine) - dot3(*left_parts, c_high[...], c_low[...])
    right = dot3(*split(right), b_high[...], b_low[...])
    right_parts = split(right)
    panel = left.shape[1]
    high_ref[:, :panel], low_ref[:, :panel] = left_parts
    high_ref[:, panel:], low_ref[:, panel:] = right_parts
    alt_ref[...] = jnp.where(flag_ref[2] == 0, left, right)
    if first:
        old_high, old_low, old_alt = rest[3:]

        @pl.when(pl.program_id(0) == 0)
        def _():
            count = panels * part
            old_high[...] = high_ref[:count]
            old_low[...] = low_ref[:count]
            old_alt[...] = alt_ref[:count]


def lower(flags, x, band, bands, moved, factors, previous):
    blocks, _, part, width = x.shape
    panel = factors[0].shape[0]
    panels = 2
    size = blocks // bands
    group = max(g for g in range(1, size + 1) if size % g == 0 and (g * part <= 256 or g == 1))
    group = max(group, panels) if size % panels == 0 and band == 0 else group
    steps = size // group
    offset = band * steps
    whole = lambda j, *_: (0, 0)
    in_specs = [pl.BlockSpec((group, 1, part, width), lambda j, *_: (offset + j, 0, 0, 0))]
    in_specs += [pl.BlockSpec((group * part, width), lambda j, *_: (j, 0))] * 3
    in_specs += [pl.BlockSpec(factor.shape, whole) for factor in factors]
    args = [x, *moved, *factors]
    out_specs = [
        pl.BlockSpec((group * part, panels * panel), lambda j, *_: (offset + j, 0)),
        pl.BlockSpec((group * part, panels * panel), lambda j, *_: (offset + j, 0)),
        pl.BlockSpec((group * part, width), lambda j, *_: (offset + j, 0)),
    ]
    out_shape = [
        jax.ShapeDtypeStruct((blocks * part, panels * panel), jnp.bfloat16),
        jax.ShapeDtypeStruct((blocks * part, panels * panel), jnp.bfloat16),
        jax.ShapeDtypeStruct((blocks * part, width), jnp.float32),
    ]
    aliases = {}
    if previous is None:
        old = panels * part
        for shape, kind in (
            ((old, panels * panel), jnp.bfloat16),
            ((old, panels * panel), jnp.bfloat16),
            ((old, width), jnp.float32),
        ):
            out_specs.append(pl.BlockSpec(shape, whole))
            out_shape.append(jax.ShapeDtypeStruct(shape, kind))
    else:
        in_specs += [pl.BlockSpec(memory_space=pl.ANY)] * 3
        aliases = {1 + len(args) + index: index for index in range(3)}
        args += previous
    return pl.pallas_call(
        functools.partial(lower_kernel, first=previous is None, panels=panels),
        grid_spec=pltpu.PrefetchScalarGridSpec(
            num_scalar_prefetch=1, grid=(steps,), in_specs=in_specs, out_specs=out_specs
        ),
        out_shape=out_shape,
        input_output_aliases=aliases,
        cost_estimate=pl.CostEstimate(
            flops=18 * size * part * panel * panel, transcendentals=0, bytes_accessed=28 * size * part * width
        ),
        name="lower",
    )(flags, *args)


def trail_kernel(flag_ref, row_ref, slot_ref, count_ref, *refs, special):
    x_ref, l_high, l_low, u_high, u_low, front_ref, come_ref = refs[:7]
    rest = refs[7:]
    if special:
        alt_ref, corner_ref, rest = rest[0], rest[1], rest[2:]
    o_ref = rest[-1]
    group, _, part, width = x_ref.shape
    band = pl.program_id(0)
    value = x_ref[...].reshape(group * part, width) - dot3(l_high[...], l_low[...], u_high[0], u_low[0])
    if special:
        chosen = (flag_ref[1] > 0) & (pl.program_id(1) == 0)
        value = jnp.where(chosen, alt_ref[...], value)
    o_ref[:, 0] = value.reshape(group, part, width)

    @pl.when(band == 0)
    def _():
        for index in range(front_ref.shape[1]):
            front = front_ref[0, index]
            if special:
                front = jnp.where(chosen, corner_ref[index], front)
            o_ref[index, 0] = front

    devices, _, pair_cap, _ = come_ref.shape
    base = band * (devices * pair_cap)

    def body(index, _):
        spot = row_ref[base + index]
        slot = slot_ref[base + index]
        o_ref[spot // part, 0, pl.ds(spot % part, 1), :] = come_ref[slot // pair_cap, 0, pl.ds(slot % pair_cap, 1), :]
        return 0

    lax.fori_loop(0, count_ref[band], body, 0)


def trail(flags, tables, x, col, low, upper, front, come, special, previous, bands):
    blocks, _, part, width = x.shape
    per, total, _ = upper[0].shape
    group = blocks // bands
    in_specs = [
        pl.BlockSpec((group, 1, part, width), lambda j, i, *_: (j, col + i, 0, 0)),
        pl.BlockSpec((group * part, total), lambda j, i, *_: (j, 0)),
        pl.BlockSpec((group * part, total), lambda j, i, *_: (j, 0)),
        pl.BlockSpec((1, total, width), lambda j, i, *_: (i, 0, 0)),
        pl.BlockSpec((1, total, width), lambda j, i, *_: (i, 0, 0)),
        pl.BlockSpec((1,) + front.shape[1:], lambda j, i, *_: (i, 0, 0, 0)),
        pl.BlockSpec((come.shape[0], 1) + come.shape[2:], lambda j, i, *_: (0, i, 0, 0)),
    ]
    args = [x, *low, *upper, front, come]
    if special is not None:
        alt, corner = special
        in_specs.append(pl.BlockSpec((group * part, width), lambda j, i, *_: (j, 0)))
        in_specs.append(pl.BlockSpec(corner.shape, lambda j, i, *_: (0, 0, 0)))
        args += [alt, corner]
    aliases = {}
    if previous is not None:
        in_specs.append(pl.BlockSpec(memory_space=pl.ANY))
        args.append(previous)
        aliases = {4 + len(args) - 1: 0}
    return pl.pallas_call(
        functools.partial(trail_kernel, special=special is not None),
        grid_spec=pltpu.PrefetchScalarGridSpec(
            num_scalar_prefetch=4,
            grid=(bands, per),
            in_specs=in_specs,
            out_specs=pl.BlockSpec((group, 1, part, width), lambda j, i, *_: (j, col + i, 0, 0)),
        ),
        out_shape=jax.ShapeDtypeStruct(x.shape, jnp.float32),
        input_output_aliases=aliases,
        cost_estimate=pl.CostEstimate(
            flops=6 * per * blocks * part * total * width,
            transcendentals=0,
            bytes_accessed=16 * per * blocks * part * width,
        ),
        name="trail",
    )(flags, *tables, *args)


def ring_gather(own, devices):
    order = list(range(0, devices, 2)) + list(range(devices - 1, 0, -2))
    forward = [(order[i], order[(i + 1) % devices]) for i in range(devices)]
    backward = [(b, a) for a, b in forward]
    ahead = behind = own
    ahead_list, behind_list = [], []
    for _ in range(devices // 2 - 1):
        ahead = lax.ppermute(ahead, "prow", forward)
        behind = lax.ppermute(behind, "prow", backward)
        ahead_list.append(ahead)
        behind_list.append(behind)
    if own.shape[0] % 2 == 0:
        half = own.shape[0] // 2
        left, right = ahead[:half], behind[half:]
    else:
        half = own.shape[2] // 2
        left, right = ahead[:, :, :half], behind[:, :, half:]
    left = lax.ppermute(left, "prow", forward)
    right = lax.ppermute(right, "prow", backward)
    return [own, *ahead_list, *reversed(behind_list), left, right]


def row_moves(block, col_index, col_devices):
    moving = crossed = block
    for hop in range(1, col_devices // 2):
        moving = lax.ppermute(moving, "pcol", [(2 * hop - 2, 2 * hop), (2 * hop - 1, 2 * hop + 1)])
        crossed = moving if hop == 1 else jnp.where(col_index // 2 == hop, moving, crossed)
    home = lax.ppermute(block, "pcol", [(0, 1), (1, 0)])
    rest = [(i, i ^ 1) for i in range(2, col_devices)]
    if not rest:
        return crossed, home, home
    swap = lax.ppermute(crossed, "pcol", rest)
    return crossed, home, swap


def panel_pair(block, col_index, col_devices):
    crossed, home, swap = row_moves(block, col_index, col_devices)
    at_home = col_index < 2
    mine = jnp.where(at_home, block, crossed)
    other = jnp.where(at_home, home, swap)
    even = col_index % 2 == 0
    return jnp.where(even, mine, other), jnp.where(even, other, mine)


def chunking(cols):
    if cols < 4:
        return [1] * cols
    middle = cols // 2
    return [1, middle, cols - 1 - middle]


def grouping(chunks):
    return [[chunk] for chunk in range(chunks)]


def fast(x, place, column, tables, lower_inv, upper_inv, sizes):
    panel, part, devices, cap, pair_cap, bands, rows = sizes
    send_at, out_at, in_tables = tables
    blocks, cols, _, width = x.shape
    panels = lower_inv.shape[0]
    row_index = lax.axis_index("prow")
    col_index = lax.axis_index("pcol")
    col_devices = lax.axis_size("pcol")
    widths = chunking(cols)
    chunks = [(sum(widths[:i]), per) for i, per in enumerate(widths)]
    flags = jnp.stack([row_index, col_index < panels, col_index, col_index < 2, col_index % 2 == 0]).astype(jnp.int32)
    raw = []
    for band in range(bands):
        block = x[band * (blocks // bands) : (band + 1) * (blocks // bands), 0].reshape(rows, width)
        raw.append(row_moves(block, col_index, col_devices))
    gathered = []
    for col, per in chunks:
        own = pack(send_at, x, col, per, cap)
        gathered.append(ring_gather(own, devices))
    head, sent = unpack(flags, place, gathered[0], cap, devices, panel)
    parts = select(column, lower_inv, upper_inv, devices * cap)
    s_high, s_low, pick, v_high, v_low = parts[:5]
    upper_parts = parts[5:]
    moved = row_moves(sent, col_index, col_devices)
    t_high, t_low, c_high, c_low, front_corner = corner(flags, sent, moved, lower_inv, upper_parts[:2], head, part)
    low = old = None
    for band in range(bands):
        outs = lower(flags, x, band, bands, raw[band], [*upper_parts, c_high, c_low], low)
        low = outs[:3]
        old = outs[3:] if band == 0 else old
    alt = low[2]
    factors = [s_high, s_low, pick, t_high, t_low, v_high, v_low]
    result = None
    for group in grouping(len(chunks)):
        col = chunks[group[0]][0]
        u_high, u_low, front, send = solve(
            flags,
            out_at,
            factors,
            old[:2],
            x,
            col,
            [gathered[chunk] for chunk in group],
            old[2] if col == 0 else None,
            cap,
            devices,
            pair_cap,
            panels,
        )
        come = lax.all_to_all(send, "prow", 0, 0, tiled=True)
        special = (alt, front_corner) if col == 0 else None
        result = trail(flags, in_tables, x, col, low[:2], (u_high, u_low), front, come, special, result, bands)
    return result


def slow(x, wanted, came_from, pivots, lower_inv, upper_inv, result, sizes):
    panel, part, devices = sizes[:3]
    blocks, cols, _, width = x.shape
    total = wanted.shape[0]
    x = plain(x)
    row_index = lax.axis_index("prow")
    col_index = lax.axis_index("pcol")
    col_devices = lax.axis_size("pcol")
    rows = jnp.arange(blocks, dtype=jnp.int32)[:, None] * panel + jnp.arange(part, dtype=jnp.int32)[None, :]
    rows = (rows + row_index * part).reshape(-1)
    spots = jnp.where(came_from >= 0, pivots, blocks * panel)
    source = jnp.full((blocks * panel,), -1, jnp.int32).at[spots].set(came_from, mode="drop")[rows]
    needed = jnp.concatenate([wanted, jnp.arange(total, dtype=jnp.int32)])
    mine = (needed % panel // part == row_index)[:, None]
    spot = needed // panel * part + needed % part
    around = [(i, (i + 1) % devices) for i in range(devices)]

    def swapped(col):
        here = lax.dynamic_index_in_dim(x, col, 1, False).reshape(blocks * part, width)
        moving = jnp.where(mine, here[spot], 0.0)

        def hop(_, carry):
            moving, gathered = carry
            moving = lax.ppermute(moving, "prow", around)
            return moving, gathered + moving

        _, gathered = lax.fori_loop(0, devices - 1, hop, (moving, moving))
        head = gathered[:total]
        return head, jnp.where((source >= 0)[:, None], gathered[total:][jnp.maximum(source, 0)], here)

    head, body = swapped(0)
    raw = panel_pair(body, col_index, col_devices)
    corner = panel_pair(head, col_index, col_devices)
    low_top = product(corner[0][panel:], upper_inv[0])
    up_side = product(lower_inv[0], corner[1][:panel])
    low_first = product(raw[0], upper_inv[0])
    low_second = product(raw[1] - product(low_first, up_side), upper_inv[1])

    def column(col, result):
        head, body = swapped(col)
        upper = product(lower_inv[0], head[:panel])
        reduced = head[panel:] - product(low_top, upper)
        second = product(lower_inv[1], reduced)
        body = body - product(low_first, upper) - product(low_second, second)
        left = (col == 0) & (col_index == 0)
        right = (col == 0) & (col_index == 1)
        body = jnp.where(left, low_first, jnp.where(right, low_second, body))
        upper = jnp.where(left, head[:panel], upper)
        second = jnp.where(left, low_top, jnp.where(right, reduced, second))
        own = [lax.dynamic_slice_in_dim(side, row_index * part, part, 0) for side in (upper, second)]
        body = jnp.concatenate([*own, body[2 * part :]], axis=0)
        return plain(lax.dynamic_update_index_in_dim(plain(result), body.reshape(blocks, part, width), col, 1))

    return lax.fori_loop(0, cols, column, result)


def local(matrix, pivots, lower_inv, upper_inv):
    row_blocks, row_part, _, _ = matrix.shape
    panels, panel = pivots.shape
    devices = lax.axis_size("prow")
    total = panels * panel
    mean = total / devices
    cap = -(-int(mean + 2.75 * math.sqrt(mean)) // 8) * 8
    pair_mean = mean / devices
    pair_cap = -(-int(pair_mean + 4 * math.sqrt(pair_mean)) // 8) * 8
    bands = 2 if row_blocks % 2 == 0 else 1
    sizes = (panel, row_part, devices, cap, pair_cap, bands, row_blocks // bands * row_part)
    x = matrix.transpose(0, 2, 1, 3)
    me = lax.axis_index("prow").astype(jnp.int32).reshape(1)
    send_at, place, column, out_at, in_rows, in_slots, counts, over, wanted, came_from = routing(me, pivots, sizes)
    tables = (send_at[0], out_at[0], (in_rows[0], in_slots[0], counts[0]))
    result = fast(x, place[0], column, tables, lower_inv, upper_inv, sizes)

    def again(carry):
        _, result = carry
        result = slow(x, wanted[0], came_from[0], pivots.reshape(-1), lower_inv, upper_inv, result, sizes)
        return jnp.int32(-1), plain(result)

    _, result = lax.while_loop(lambda carry: carry[0] >= 0, again, (over[0, 0], plain(result)))
    return result.transpose(0, 2, 1, 3)


def solution(mesh):
    return jax.shard_map(
        local,
        mesh=mesh,
        in_specs=(P(None, "prow", None, "pcol"), P(), P(), P()),
        out_specs=P(None, "prow", None, "pcol"),
        check_vma=False,
    )
```
